128 devices in a mesh: band: 32 (over z, y, core), lon: 4 (over x).
Axes of the slice: x: 4, y: 4, z: 4, core: 2. Of those that a mesh axis runs over, the one named last changes fastest.
Arguments:
- source: bfloat16 [16384, 8, 128], P(('band', 'lon')), may hold values from -6 to 6
- routes: int32 [16384, 2], P(('band', 'lon')), may hold values from 0 to 11, as said below
- slot_weights: bfloat16 [128, 12, 32, 128, 128], P(('band', 'lon')), may hold values from -0.5 to 0.5
- window: int32 [128, 12, 32], P(('band', 'lon')), may hold values from 0 to 255
- stem_weight: bfloat16 [9, 8, 128], replicated, may hold values from -0.75 to 0.75
- stem_bias: float32 [128], replicated, may hold values from -3 to 3
- mix_weight: bfloat16 [9, 128, 128], replicated, may hold values from -0.1875 to 0.1875
- mix_bias: float32 [128], replicated, may hold values from -3 to 3
Outputs:
- features: bfloat16 [2048, 2048, 128], P('band', 'lon')
The draws below stay inside these ranges and needn't reach their ends.
Inputs may be any that keep to these rules, and one draw needn't show every extreme that they name: `routes`: each cell block names 2 different codes, never a band outside the grid. Among one device's blocks no code is named more than 32 times, and the device's own tile (code 4) exactly 32 times except in the first and last band. A device of another band names only longitude offsets 0, 1 and 3. A device of the first band names each code of band offsets 0 and +1 exactly 32 times; one of the last band each code of band offsets -1 and 0 exactly 32 times.
All inputs are finite; a program needn't handle non-finite values.
Results may differ from the reference program's by a relative error of at most 0.0056.
Values may be sent and summed in bfloat16 or wider, within the bound.
A program may use at most 128 MiB of HBM per device.

```python
import jax
import jax.numpy as jnp
from jax import lax

F = 8
CH = 128
CB = 128
PIX = 128
TOP = 2
ROWS_DEV = 64
COLS_DEV = 512
NBR = 12
BLK_DEV = 128
CAP = 32
NWIN = 256
TOTAL_BLK = 16384
LAT = 2048
LONG = 2048
N_BAND = 32
N_LON = 4
DEVICES = 128


def draw_routes(key, part):
    devices = DEVICES
    n_band = devices // N_LON
    nbr = 3 * N_LON
    entries = BLK_DEV * TOP
    key_picks = jax.random.fold_in(key, 11)
    key_flip = jax.random.fold_in(key, 12)
    key_order = jax.random.fold_in(key, 13)
    device_ids = jnp.arange(devices, dtype=jnp.int32)
    band = device_ids // N_LON
    code = jnp.arange(nbr, dtype=jnp.int32)
    offset_band = code // N_LON - 1
    offset_lon = code % N_LON
    near = (offset_lon == 0) | (offset_lon == 1) | (offset_lon == N_LON - 1)
    others = near & (code != N_LON)
    other_index = jnp.cumsum(others.astype(jnp.int32)) - 1
    picks = jax.random.randint(key_picks, (devices, CAP), 0, 8, dtype=jnp.int32)
    matches = (picks[:, :, None] == other_index[None, None, :]) & others[None, None, :]
    taken = jnp.sum(matches.astype(jnp.int32), axis=1)
    interior = jnp.where(near, CAP, 0).astype(jnp.int32)[None, :] - taken
    first_band = jnp.where(offset_band >= 0, CAP, 0).astype(jnp.int32)
    last_band = jnp.where(offset_band <= 0, CAP, 0).astype(jnp.int32)
    counts = jnp.where((band == 0)[:, None], first_band[None, :], jnp.where((band == n_band - 1)[:, None], last_band[None, :], interior))
    bounds = jnp.cumsum(counts, axis=1)
    entry = jnp.arange(entries, dtype=jnp.int32)
    ordered = jnp.sum((bounds[:, None, :] <= entry[None, :, None]).astype(jnp.int32), axis=2)
    paired = jnp.stack([ordered[:, :BLK_DEV], ordered[:, BLK_DEV:]], axis=2)
    flip = jax.random.randint(key_flip, (devices, BLK_DEV), 0, 2, dtype=jnp.int32)
    paired = jnp.where((flip == 1)[:, :, None], paired[:, :, ::-1], paired)
    scores = jax.random.randint(key_order, (devices, BLK_DEV), 0, 1 << 20, dtype=jnp.int32) * BLK_DEV + jnp.arange(BLK_DEV, dtype=jnp.int32)[None, :]
    order = jnp.argsort(scores, axis=1)
    paired = jnp.take_along_axis(paired, order[:, :, None], axis=1)
    return paired.reshape(devices * BLK_DEV, TOP).astype(jnp.int32)


def touch_ends(values, own_key, low, high):
    extent = values.shape
    spot = [jax.random.randint(jax.random.fold_in(own_key, axis), (), 0, extent[axis]) for axis in range(len(extent))]
    values = values.at[tuple(spot)].set(low)
    longest = extent.index(max(extent))
    spot[longest] = (spot[longest] + 1) % extent[longest]
    return values.at[tuple(spot)].set(high)


def steps_of(rng, shape, split, low, high):
    def one(position, parts):
        heights = jax.random.uniform(jax.random.fold_in(jax.random.fold_in(rng, 6), position), (parts,), jnp.float32, low / len(split), high / len(split))
        return jnp.repeat(jnp.exp(heights), shape[position] // parts).reshape((-1,) + (1,) * (len(shape) - position - 1))

    level = one(*split[0])
    for cut in split[1:]:
        level = level * one(*cut)
    return level


def bell_draw(own_key, extent, scale, most, split=(), held_as=jnp.bfloat16):
    drawn = jax.random.normal(own_key, extent, jnp.float32) * scale
    if len(split) > 0:
        drawn = steps_of(own_key, extent, split, -0.22, 0.18) * drawn
    return jnp.clip(drawn, min=-most, max=most).astype(held_as)


def setup_inputs(seed: int = 0) -> dict:
    streams_of = jax.random.split(jax.random.key(seed), 9)
    source = bell_draw(streams_of[0], (TOTAL_BLK, F, CB), 1.0, 6.0, ((0, 128),))
    routes = draw_routes(jax.random.fold_in(streams_of[8], 71), 0)
    slot_weights = bell_draw(streams_of[2], (DEVICES, NBR, CAP, CB, PIX), CB ** -0.5, 0.5, ((0, 128),))
    window = touch_ends(jax.random.randint(streams_of[3], (DEVICES, NBR, CAP), 0, NWIN), jax.random.fold_in(streams_of[3], 1), 0, NWIN - 1).astype(jnp.int32)
    stem_weight = bell_draw(streams_of[4], (9, F, CH), (9 * F) ** -0.5, 0.75)
    stem_bias = bell_draw(streams_of[5], (CH,), 0.5, 3.0, (), jnp.float32)
    mix_weight = bell_draw(streams_of[6], (9, CH, CH), (9 * CH) ** -0.5, 0.1875)
    mix_bias = bell_draw(streams_of[7], (CH,), 0.5, 3.0, (), jnp.float32)
    return dict(source=source, routes=routes, slot_weights=slot_weights, window=window, stem_weight=stem_weight, stem_bias=stem_bias, mix_weight=mix_weight, mix_bias=mix_bias)


def reference(source, routes, slot_weights, window, stem_weight, stem_bias, mix_weight, mix_bias):
    devices = N_BAND * N_LON
    nbr = 3 * N_LON
    entries = BLK_DEV * TOP
    blocks = source.reshape(devices, BLK_DEV, F * CB)
    codes = routes.reshape(devices, entries)

    def pack(pair):
        dest, blk = pair
        onehot = (dest[:, None] == jnp.arange(nbr, dtype=jnp.int32)[None, :]).astype(jnp.int32)
        before = jnp.cumsum(onehot, axis=0) - onehot
        rank = jnp.sum(before * onehot, axis=1)
        slot = dest * CAP + rank
        select = (jnp.arange(nbr * CAP, dtype=jnp.int32)[:, None] == slot[None, :]).astype(jnp.bfloat16)
        repeated = jnp.repeat(blk, TOP, axis=0)
        return jnp.dot(select, repeated, preferred_element_type=jnp.float32).astype(jnp.bfloat16)

    outgoing = lax.map(pack, (codes, blocks)).reshape(devices, nbr, CAP, F * CB)

    def one_tile(target):
        band_t = target // N_LON
        lon_t = target % N_LON
        code = jnp.arange(nbr, dtype=jnp.int32)
        src_band = band_t - (code // N_LON - 1)
        src_lon = (lon_t - code % N_LON) % N_LON
        valid = (src_band >= 0) & (src_band < N_BAND)
        src = (jnp.clip(src_band, 0, N_BAND - 1) * N_LON + src_lon).astype(jnp.int32)
        incoming = outgoing[src, code]
        incoming = jnp.where(valid[:, None, None], incoming, jnp.zeros_like(incoming))
        incoming = incoming.reshape(nbr, CAP, F, CB).astype(jnp.float32)
        weights = slot_weights[target].astype(jnp.float32)
        contrib = jnp.einsum('qcfk,qckp->qcfp', incoming, weights).astype(jnp.bfloat16)
        place = (jnp.arange(NWIN, dtype=jnp.int32)[:, None] == window[target].reshape(-1)[None, :]).astype(jnp.bfloat16)
        summed = jnp.dot(place, contrib.reshape(nbr * CAP, F * PIX), preferred_element_type=jnp.float32)
        tile = summed.reshape(ROWS_DEV, COLS_DEV // PIX, F, PIX).transpose(2, 0, 1, 3)
        return tile.reshape(F, ROWS_DEV, COLS_DEV).astype(jnp.bfloat16)

    tiles = lax.map(one_tile, jnp.arange(devices, dtype=jnp.int32))
    field = tiles.reshape(N_BAND, N_LON, F, ROWS_DEV, COLS_DEV).transpose(2, 0, 3, 1, 4).reshape(F, LAT, LONG)
    padded = jnp.pad(field, ((0, 0), (2, 2), (0, 0)))
    padded = jnp.concatenate([padded[:, :, -2:], padded, padded[:, :, :2]], axis=2)
    stem_f = stem_weight.astype(jnp.float32)

    def one_band(band_index):
        piece = lax.dynamic_slice_in_dim(padded, band_index * ROWS_DEV, ROWS_DEV + 4, axis=1).astype(jnp.float32)
        total = jnp.zeros((ROWS_DEV + 2, LONG + 2, CH), jnp.float32)
        for tap in range(9):
            a, b = tap // 3, tap % 3
            total = total + jnp.einsum('fhw,fc->hwc', piece[:, a:a + ROWS_DEV + 2, b:b + LONG + 2], stem_f[tap])
        hidden = jax.nn.silu(total + stem_bias)
        rows = band_index * ROWS_DEV - 1 + jnp.arange(ROWS_DEV + 2, dtype=jnp.int32)
        valid = (rows >= 0) & (rows < LAT)
        hidden = jnp.where(valid[:, None, None], hidden, 0.0).astype(jnp.bfloat16)
        result = jnp.zeros((ROWS_DEV, LONG, CH), jnp.float32)
        for tap in range(9):
            a, b = tap // 3, tap % 3
            result = result + jnp.dot(hidden[a:a + ROWS_DEV, b:b + LONG], mix_weight[tap], preferred_element_type=jnp.float32)
        return (result + mix_bias).astype(jnp.bfloat16)

    bands = lax.map(one_band, jnp.arange(N_BAND, dtype=jnp.int32))
    return bands.reshape(LAT, LONG, CH)
```

```python
import jax
import jax.numpy as jnp
from jax import lax
from jax.experimental import pallas as pl
from jax.experimental.pallas import tpu as pltpu
from jax.sharding import PartitionSpec as P

ROWS_DEV = 64
COLS_DEV = 512


def shifted(block, axis, distance):
    devices = range(lax.axis_size(axis))
    route = [(i - distance, i) for i in devices if i - distance in devices]
    return lax.ppermute(block, axis, route)


def extended(block, sides, width, periodic):
    for axis, dim in sides:
        count = lax.axis_size(axis)
        forward = [(i, i + 1) for i in range(count - 1)]
        if periodic:
            forward.append((count - 1, 0))
        backward = [(target, source) for source, target in forward]
        low = lax.ppermute(
            lax.slice_in_dim(block, block.shape[dim] - width, None, axis=dim), axis, forward
        )
        high = lax.ppermute(lax.slice_in_dim(block, 0, width, axis=dim), axis, backward)
        block = jnp.concatenate([low, block, high], axis=dim)
    return block


MCH = 256

def conv_kernel(flags, ft, sw, sb, mw, mb, out, tmat, mmat, lhs3, tmp, h32, r0, r1, r2, o0, o1, o2, sems):
    f32, bf16 = jnp.float32, jnp.bfloat16
    sw32 = sw[...].astype(f32)
    for j in range(7):
        for y in range(2):
            top = 2 * j + y
            for b in range(3):
                pieces = []
                if top > 0:
                    pieces.append(jnp.zeros((8 * top, 128), f32))
                for a in range(3):
                    pieces.append(sw32[(3 * a + b) * 8 : (3 * a + b) * 8 + 8])
                if top < 13:
                    pieces.append(jnp.zeros((8 * (13 - top), 128), f32))
                tmat[j, b * 128 : b * 128 + 128, y * 128 : y * 128 + 128] = jnp.concatenate(pieces, axis=0).astype(bf16)
    for r in range(4):
        for b in range(3):
            for o in range(2):
                a = r - o
                block = mw[3 * a + b] if 0 <= a <= 2 else jnp.zeros((128, 128), bf16)
                mmat[(r * 3 + b) * 128 : (r * 3 + b) * 128 + 128, o * 128 : o * 128 + 128] = block
    for k in range(5):
        tmp[...] = ft[k].astype(f32)
        for b in range(3):
            lhs3[k, :, b * 128 : b * 128 + 128] = tmp[b : b + 520].astype(bf16)

    hb = sb[...] * 0.5
    bias = mb[...]
    first, last = flags[0], flags[1]

    def stem(pair, ring):
        k = pair // 7
        j = pair - k * 7
        acc = jnp.dot(lhs3[k], tmat[j], preferred_element_type=f32)
        for y in range(2):
            u = acc[:, y * 128 : y * 128 + 128] * 0.5 + hb
            h = u + u * jnp.tanh(u)
            row = 2 * pair + y
            gone = jnp.logical_or(jnp.logical_and(first == 1, row == 0), jnp.logical_and(last == 1, row == 65))
            h32[y] = h * jnp.where(gone, 0.0, 1.0)
            for b in range(3):
                ring[y, :, b * 128 : b * 128 + 128] = h32[y, b : b + 512].astype(bf16)

    def mix(p, lo, hi, ob):
        for m in range(0, 512, MCH):
            lhs = jnp.concatenate([lo[0, m : m + MCH], lo[1, m : m + MCH], hi[0, m : m + MCH], hi[1, m : m + MCH]], axis=1)
            acc = jnp.dot(lhs, mmat[...], preferred_element_type=f32)
            ob[0, m : m + MCH] = (acc[:, :128] + bias).astype(bf16)
            ob[1, m : m + MCH] = (acc[:, 128:] + bias).astype(bf16)

    rings = (r0, r1, r2)
    obs = (o0, o1, o2)
    stem(jnp.int32(0), r0)
    stem(jnp.int32(1), r1)

    def put(p, i):
        return pltpu.make_async_copy(obs[i], out.at[pl.ds(2 * p, 2)], sems.at[i])

    def body(t, carry):
        for i in range(3):
            p = 3 * t + i

            @pl.when(t > 0)
            def _():
                put(p - 3, i).wait()

            mix(p, rings[i], rings[(i + 1) % 3], obs[i])
            stem(p + 2, rings[(i + 2) % 3])
            put(p, i).start()
        return carry

    lax.fori_loop(0, 10, body, 0)
    for i in range(2):
        put(27 + i, i).wait()
        mix(30 + i, rings[i], rings[(i + 1) % 3], obs[i])
        if i == 0:
            stem(jnp.int32(32), r2)
        put(30 + i, i).start()
    put(29, 2).wait()
    put(30, 0).wait()
    put(31, 1).wait()


def conv(flags, ft, sw, sb, mw, mb):
    V = pltpu.VMEM
    bf16, f32 = jnp.bfloat16, jnp.float32
    vm = pl.BlockSpec(memory_space=pltpu.VMEM)
    return pl.pallas_call(
        conv_kernel,
        out_shape=jax.ShapeDtypeStruct((64, 512, 128), bf16),
        in_specs=[pl.BlockSpec(memory_space=pltpu.SMEM)] + [vm] * 5,
        out_specs=pl.BlockSpec(memory_space=pl.ANY),
        scratch_shapes=[
            V((7, 384, 256), bf16), V((1536, 256), bf16), V((5, 520, 384), bf16),
            V((528, 128), f32), V((2, 520, 128), f32),
            V((2, 512, 384), bf16), V((2, 512, 384), bf16), V((2, 512, 384), bf16),
            V((2, 512, 128), bf16), V((2, 512, 128), bf16), V((2, 512, 128), bf16),
            pltpu.SemaphoreType.DMA((3,)),
        ],
        compiler_params=pltpu.CompilerParams(vmem_limit_bytes=60 * 1024 * 1024),
        name="conv",
    )(flags, ft, sw, sb, mw, mb)


def on_device(source, routes, slot_weights, window, stem_weight, stem_bias, mix_weight, mix_bias):
    n_lon = lax.axis_size("lon")
    lon_here = lax.axis_index("lon")
    blk_dev, fields, cells = source.shape
    nbr = slot_weights.shape[1]
    cap = slot_weights.shape[2]
    pixels = slot_weights.shape[4]
    top = routes.shape[1]
    rows = ROWS_DEV
    cols = COLS_DEV
    nwin = rows * cols // pixels
    flat_dest = routes.reshape(-1)
    onehot = (flat_dest[:, None] == jnp.arange(nbr, dtype=jnp.int32)[None, :]).astype(jnp.int32)
    before = jnp.cumsum(onehot, axis=0) - onehot
    rank = jnp.sum(before * onehot, axis=1)
    target_slot = flat_dest * cap + rank
    select = (jnp.arange(nbr * cap, dtype=jnp.int32)[:, None] == target_slot[None, :]).astype(
        jnp.bfloat16
    )
    repeated = jnp.repeat(source.reshape(blk_dev, fields * cells), top, axis=0)
    outgoing = jnp.dot(select, repeated, preferred_element_type=jnp.float32).astype(jnp.bfloat16)
    outgoing = outgoing.reshape(3, n_lon, cap, fields, cells)
    lanes = jnp.arange(n_lon, dtype=jnp.int32)
    to_absolute = (lanes - lon_here) % n_lon
    to_relative = (lon_here - lanes) % n_lon
    absolute = jnp.take(outgoing, to_absolute, axis=1)
    arrived = lax.all_to_all(absolute, "lon", split_axis=1, concat_axis=1, tiled=True)
    arrived = jnp.take(arrived, to_relative, axis=1)
    from_north = shifted(arrived[0], "band", -1)
    from_south = shifted(arrived[2], "band", 1)
    incoming = jnp.stack([from_north, arrived[1], from_south], axis=0)
    incoming = incoming.reshape(nbr, cap, fields, cells)
    contrib = jnp.einsum(
        "qcfk,qckp->qcfp", incoming, slot_weights[0], preferred_element_type=jnp.float32
    ).astype(jnp.bfloat16)
    place = (jnp.arange(nwin, dtype=jnp.int32)[:, None] == window[0].reshape(-1)[None, :]).astype(
        jnp.bfloat16
    )
    summed = jnp.dot(
        place, contrib.reshape(nbr * cap, fields * pixels), preferred_element_type=jnp.float32
    )
    field = summed.reshape(rows, cols // pixels, fields, pixels).transpose(2, 0, 1, 3)
    field = field.reshape(fields, rows, cols).astype(jnp.bfloat16)
    with_rows = extended(field, (("band", 1),), 2, False)
    full = extended(with_rows, (("lon", 2),), 2, True)
    full = jnp.pad(full, ((0, 0), (0, 4), (0, 12)))
    windows = jnp.stack([full[:, 14 * k : 14 * k + 16] for k in range(5)], axis=0)
    windows = windows.transpose(0, 3, 2, 1).reshape(5, cols + 16, 16 * fields)
    band = lax.axis_index("band")
    flags = jnp.stack([band == 0, band == lax.axis_size("band") - 1]).astype(jnp.int32)
    return conv(
        flags,
        windows,
        stem_weight.reshape(72, 128),
        stem_bias.reshape(1, 128),
        mix_weight,
        mix_bias.reshape(1, 128),
    )


def solution(mesh):
    in_specs = (
        P(("band", "lon"), None, None),
        P(("band", "lon"), None),
        P(("band", "lon"), None, None, None, None),
        P(("band", "lon"), None, None),
        P(),
        P(),
        P(),
        P(),
    )
    out_specs = P("band", "lon", None)
    return jax.shard_map(
        on_device, mesh=mesh, in_specs=in_specs, out_specs=out_specs, check_vma=False
    )
```

```python
import jax
import jax.numpy as jnp
from jax import lax
from jax.experimental import pallas as pl
from jax.experimental.pallas import tpu as pltpu
from jax.sharding import PartitionSpec as P

NT = (((1,), (1,)), ((), ()))


def gather_kernel(src, routes, window, weights, ft, wv, s32, o32, sendb, recvb, c32, place, fs32, fe, colr, coll,
                  lc, ln, ls, rc, rn, rs, w_sem, send_sem, recv_sem, hs_sem, hr_sem):
    f32, bf16 = jnp.float32, jnp.bfloat16
    n_band, n_lon = lax.axis_size("band"), lax.axis_size("lon")
    band, lon = lax.axis_index("band"), lax.axis_index("lon")
    barrier = pltpu.get_barrier_semaphore()

    def there(q):
        return {"band": band + (q // 4 - 1), "lon": lax.rem(lon + q % 4, n_lon)}

    def inside(b):
        return jnp.logical_and(b >= 0, b < n_band)

    def edge(b):
        return jnp.logical_or(b == 0, b == n_band - 1)

    def sends(q):
        ok = inside(band + (q // 4 - 1))
        return jnp.logical_and(ok, edge(band)) if q % 4 == 2 else ok

    def gets(q):
        origin = band - (q // 4 - 1)
        return jnp.logical_and(inside(origin), edge(origin)) if q % 4 == 2 else inside(origin)

    def greets(q):
        target = band + (q // 4 - 1)
        ok = inside(target)
        return jnp.logical_and(ok, jnp.logical_or(edge(band), edge(target))) if q % 4 == 2 else ok

    others = [q for q in range(12) if q != 4]
    count = jnp.int32(0)
    for q in others:
        @pl.when(greets(q))
        def _():
            pl.semaphore_signal(barrier, inc=1, device_id=there(q), device_id_type=pl.DeviceIdType.MESH)
        count = count + greets(q).astype(jnp.int32)

    order = (4, 0, 8, 5, 7, 1, 3, 9, 11, 6, 2, 10)

    def fetch(q):
        return pltpu.make_async_copy(weights.at[q], wv.at[q], w_sem.at[q])

    for q in order:
        fetch(q).start()

    code = lax.broadcasted_iota(jnp.int32, (128, 128), 1)
    block = lax.broadcasted_iota(jnp.int32, (128, 128), 0)
    names = jnp.logical_or(routes[:, 0:1] == code, routes[:, 1:2] == code)
    earlier = (code < block).astype(f32).astype(bf16)
    rank = jnp.dot(earlier, names.astype(f32).astype(bf16), preferred_element_type=f32)
    ranked = jnp.where(names, rank, -1.0).T
    slot = lax.broadcasted_iota(jnp.int32, (32, 128), 0).astype(f32)
    select = jnp.concatenate(
        [(jnp.broadcast_to(ranked[q : q + 1], (32, 128)) == slot).astype(f32) for q in range(12)], axis=0
    ).astype(bf16)
    s32[...] = src[...].astype(f32).reshape(1024, 128)
    for f in range(0, 8, 2):
        planes = jnp.concatenate(
            [s32[pl.ds(f + i, 128, stride=8), :].astype(bf16) for i in range(2)], axis=1
        )
        packed = jnp.dot(select, planes, preferred_element_type=f32)
        for i in range(2):
            o32[pl.ds(f + i, 384, stride=8), :] = packed[:, i * 128 : i * 128 + 128]
    for q in range(12):
        sendb[q] = o32[q * 256 : q * 256 + 256, :].astype(bf16)

    pl.semaphore_wait(barrier, count)

    def route(q):
        return pltpu.make_async_remote_copy(
            src_ref=sendb.at[q], dst_ref=recvb.at[q], send_sem=send_sem.at[q], recv_sem=recv_sem.at[q],
            device_id=there(q), device_id_type=pl.DeviceIdType.MESH,
        )

    for q in (2, 6, 10, 1, 3, 9, 11, 5, 7, 0, 8):
        @pl.when(sends(q))
        def _():
            route(q).start()

    spot = lax.broadcasted_iota(jnp.int32, (256, 384), 0)
    wanted = lax.rem(spot, 64) * 4 + lax.div(spot, 64)
    place[...] = (jnp.broadcast_to(window[...], (256, 384)) == wanted).astype(f32).astype(bf16)
    zero_rows = jnp.zeros((16, 512), bf16)
    zero_tile = jnp.zeros((16, 128), bf16)
    fe[544:576, :] = jnp.zeros((32, 512), bf16)

    @pl.when(band == 0)
    def _():
        fe[0:16, :] = zero_rows
        ln[...] = zero_tile
        rn[...] = zero_tile

    @pl.when(band == n_band - 1)
    def _():
        fe[528:544, :] = zero_rows
        ls[...] = zero_tile
        rs[...] = zero_tile

    for q in order:
        if q == 4:
            held = sendb.at[4]
        else:
            held = recvb.at[q]

            @pl.when(gets(q))
            def _():
                route(q).wait_recv()

            @pl.when(jnp.logical_not(gets(q)))
            def _():
                recvb[q] = jnp.zeros((256, 128), bf16)

        fetch(q).wait()

        def group(g, carry):
            for i in range(8):
                row = pl.multiple_of((g * 8 + i) * 16, 16)
                col = pl.multiple_of((g * 8 + i) * 256, 256)
                both = jnp.concatenate([wv[q, pl.ds(col, 128), :], wv[q, pl.ds(col + 128, 128), :]], axis=1)
                got = jnp.dot(held[pl.ds(row, 16), :], both, preferred_element_type=f32)
                c32[pl.ds(q * 256 + row, 8), :] = got[0:8, 0:128]
                c32[pl.ds(q * 256 + row + 8, 8), :] = got[8:16, 128:256]
            return carry

        lax.fori_loop(0, 2, group, 0)

    for f in range(0, 8, 2):
        planes = jnp.concatenate(
            [c32[pl.ds(f + i, 384, stride=8), :].astype(bf16) for i in range(2)], axis=1
        )
        summed = jnp.dot(place[...], planes, preferred_element_type=f32)
        for i in range(2):
            for c in range(4):
                fs32[c, pl.ds(f + i, 64, stride=8), :] = summed[
                    c * 64 : c * 64 + 64, i * 128 : i * 128 + 128
                ]
    for c in range(4):
        fe[16:528, c * 128 : c * 128 + 128] = fs32[c].astype(bf16)

    pick_row = lax.broadcasted_iota(jnp.int32, (16, 128), 0)
    pick_col = lax.broadcasted_iota(jnp.int32, (16, 128), 1)
    pick_left = jnp.logical_and(pick_row == pick_col, pick_row < 2).astype(f32).astype(bf16)
    pick_right = (pick_col == pick_row + 112).astype(f32)
    pick_right = jnp.where(pick_row >= 14, pick_right, 0.0).astype(bf16)
    coll[...] = lax.dot_general(pick_left, fe[16:528, 0:128], NT, preferred_element_type=f32).astype(bf16)
    colr[...] = lax.dot_general(pick_right, fe[16:528, 384:512], NT, preferred_element_type=f32).astype(bf16)

    east, west = lax.rem(lon + 1, n_lon), lax.rem(lon + n_lon - 1, n_lon)
    north, south = band - 1, band + 1

    def halo(i, source, target, b, l):
        return pltpu.make_async_remote_copy(
            src_ref=source, dst_ref=target, send_sem=hs_sem.at[i], recv_sem=hr_sem.at[i],
            device_id={"band": b, "lon": l}, device_id_type=pl.DeviceIdType.MESH,
        )

    up = [
        halo(0, colr.at[:, 0:128], ls, north, east),
        halo(1, coll.at[:, 0:128], rs, north, west),
        halo(2, fe.at[16:32, :], fe.at[528:544, :], north, lon),
    ]
    down = [
        halo(3, colr.at[:, 384:512], ln, south, east),
        halo(4, coll.at[:, 384:512], rn, south, west),
        halo(5, fe.at[512:528, :], fe.at[0:16, :], south, lon),
    ]
    side = [halo(6, colr, lc, band, east), halo(7, coll, rc, band, west)]

    @pl.when(band > 0)
    def _():
        for c in up:
            c.start()

    @pl.when(band < n_band - 1)
    def _():
        for c in down:
            c.start()

    for c in side:
        c.start()

    same = (lax.broadcasted_iota(jnp.int32, (128, 128), 0) == lax.broadcasted_iota(jnp.int32, (128, 128), 1))
    same = same.astype(f32).astype(bf16)

    def turn(k):
        for t in range(4):
            ft[k, 16 + t * 128 : 144 + t * 128, :] = lax.dot_general(
                same, fe[112 * k : 112 * k + 128, t * 128 : t * 128 + 128], NT, preferred_element_type=f32
            ).astype(bf16)

    for k in (1, 2, 3):
        turn(k)

    @pl.when(band < n_band - 1)
    def _():
        for c in up:
            c.wait_recv()

    @pl.when(band > 0)
    def _():
        for c in down:
            c.wait_recv()

    for c in side:
        c.wait_recv()
    for k in (0, 4):
        turn(k)

    lane = lax.broadcasted_iota(jnp.int32, (16, 640), 1)
    blank = jnp.zeros((16, 512), f32)

    def column(c, n, s):
        mid = pltpu.roll(jnp.concatenate([c[...].astype(f32), jnp.zeros((16, 128), f32)], axis=1), 16, 1)
        top = jnp.concatenate([pltpu.roll(n[...].astype(f32), 16, 1), blank], axis=1)
        low = jnp.concatenate([blank, pltpu.roll(s[...].astype(f32), 16, 1)], axis=1)
        whole = jnp.where(lane < 16, top, jnp.where(lane < 528, mid, jnp.where(lane < 544, low, 0.0)))
        return [
            (whole if k == 0 else pltpu.roll(whole, 640 - 112 * k, 1))[:, 0:128].astype(bf16) for k in range(5)
        ]

    left, right = column(lc, ln, ls), column(rc, rn, rs)
    for k in range(5):
        ft[k, 0:16, :] = left[k]
        ft[k, 528:544, :] = right[k]

    for q in others:
        @pl.when(sends(q))
        def _():
            route(q).wait_send()

    @pl.when(band > 0)
    def _():
        for c in up:
            c.wait_send()

    @pl.when(band < n_band - 1)
    def _():
        for c in down:
            c.wait_send()

    for c in side:
        c.wait_send()


def gather(source, routes, window, weights):
    V, D = pltpu.VMEM, pltpu.SemaphoreType.DMA
    bf16, f32 = jnp.bfloat16, jnp.float32
    vm = pl.BlockSpec(memory_space=pltpu.VMEM)
    return pl.pallas_call(
        gather_kernel,
        out_shape=jax.ShapeDtypeStruct((5, 544, 128), bf16),
        in_specs=[vm, vm, vm, pl.BlockSpec(memory_space=pl.ANY)],
        out_specs=vm,
        scratch_shapes=[
            V((12, 4096, 128), bf16), V((1024, 128), f32), V((3072, 128), f32),
            V((12, 256, 128), bf16), V((12, 256, 128), bf16), V((3072, 128), f32),
            V((256, 384), bf16), V((4, 512, 128), f32), V((576, 512), bf16),
            V((16, 512), bf16), V((16, 512), bf16),
            V((16, 512), bf16), V((16, 128), bf16), V((16, 128), bf16),
            V((16, 512), bf16), V((16, 128), bf16), V((16, 128), bf16),
            D((12,)), D((12,)), D((12,)), D((8,)), D((8,)),
        ],
        compiler_params=pltpu.CompilerParams(
            collective_id=0, has_side_effects=True, vmem_limit_bytes=56 * 1024 * 1024
        ),
        name="gather",
    )(source, routes, window, weights)


MCH = 256

def conv_kernel(flags, ft, sw, sb, mw, mb, out, tmat, mmat, lhs3, tmp, h32, r0, r1, r2, o0, o1, o2, sems):
    f32, bf16 = jnp.float32, jnp.bfloat16
    sw32 = sw[...].astype(f32)
    for j in range(7):
        for y in range(2):
            top = 2 * j + y
            for b in range(3):
                pieces = []
                if top > 0:
                    pieces.append(jnp.zeros((8 * top, 128), f32))
                for a in range(3):
                    pieces.append(sw32[(3 * a + b) * 8 : (3 * a + b) * 8 + 8])
                if top < 13:
                    pieces.append(jnp.zeros((8 * (13 - top), 128), f32))
                tmat[j, b * 128 : b * 128 + 128, y * 128 : y * 128 + 128] = jnp.concatenate(pieces, axis=0).astype(bf16)
    for r in range(4):
        for b in range(3):
            for o in range(2):
                a = r - o
                block = mw[3 * a + b] if 0 <= a <= 2 else jnp.zeros((128, 128), bf16)
                mmat[(r * 3 + b) * 128 : (r * 3 + b) * 128 + 128, o * 128 : o * 128 + 128] = block
    for k in range(5):
        tmp[...] = ft[k].astype(f32)
        for b in range(3):
            lhs3[k, :, b * 128 : b * 128 + 128] = tmp[b + 14 : b + 534].astype(bf16)

    hb = sb[...] * 0.5
    bias = mb[...]
    first, last = flags[0], flags[1]

    def stem(pair, ring):
        k = pair // 7
        j = pair - k * 7
        acc = jnp.dot(lhs3[k], tmat[j], preferred_element_type=f32)
        for y in range(2):
            u = acc[:, y * 128 : y * 128 + 128] * 0.5 + hb
            h = u + u * jnp.tanh(u)
            row = 2 * pair + y
            gone = jnp.logical_or(jnp.logical_and(first == 1, row == 0), jnp.logical_and(last == 1, row == 65))
            h32[y] = h * jnp.where(gone, 0.0, 1.0)
            for b in range(3):
                ring[y, :, b * 128 : b * 128 + 128] = h32[y, b : b + 512].astype(bf16)

    def mix(p, lo, hi, ob):
        for m in range(0, 512, MCH):
            lhs = jnp.concatenate([lo[0, m : m + MCH], lo[1, m : m + MCH], hi[0, m : m + MCH], hi[1, m : m + MCH]], axis=1)
            acc = jnp.dot(lhs, mmat[...], preferred_element_type=f32)
            ob[0, m : m + MCH] = (acc[:, :128] + bias).astype(bf16)
            ob[1, m : m + MCH] = (acc[:, 128:] + bias).astype(bf16)

    rings = (r0, r1, r2)
    obs = (o0, o1, o2)
    stem(jnp.int32(0), r0)
    stem(jnp.int32(1), r1)

    def put(p, i):
        return pltpu.make_async_copy(obs[i], out.at[pl.ds(2 * p, 2)], sems.at[i])

    def body(t, carry):
        for i in range(3):
            p = 3 * t + i

            @pl.when(t > 0)
            def _():
                put(p - 3, i).wait()

            mix(p, rings[i], rings[(i + 1) % 3], obs[i])
            stem(p + 2, rings[(i + 2) % 3])
            put(p, i).start()
        return carry

    lax.fori_loop(0, 10, body, 0)
    for i in range(2):
        put(27 + i, i).wait()
        mix(30 + i, rings[i], rings[(i + 1) % 3], obs[i])
        if i == 0:
            stem(jnp.int32(32), r2)
        put(30 + i, i).start()
    put(29, 2).wait()
    put(30, 0).wait()
    put(31, 1).wait()


def conv(flags, ft, sw, sb, mw, mb):
    V = pltpu.VMEM
    bf16, f32 = jnp.bfloat16, jnp.float32
    vm = pl.BlockSpec(memory_space=pltpu.VMEM)
    return pl.pallas_call(
        conv_kernel,
        out_shape=jax.ShapeDtypeStruct((64, 512, 128), bf16),
        in_specs=[pl.BlockSpec(memory_space=pltpu.SMEM)] + [vm] * 5,
        out_specs=pl.BlockSpec(memory_space=pl.ANY),
        scratch_shapes=[
            V((7, 384, 256), bf16), V((1536, 256), bf16), V((5, 520, 384), bf16),
            V((544, 128), f32), V((2, 520, 128), f32),
            V((2, 512, 384), bf16), V((2, 512, 384), bf16), V((2, 512, 384), bf16),
            V((2, 512, 128), bf16), V((2, 512, 128), bf16), V((2, 512, 128), bf16),
            pltpu.SemaphoreType.DMA((3,)),
        ],
        compiler_params=pltpu.CompilerParams(vmem_limit_bytes=60 * 1024 * 1024),
        name="conv",
    )(flags, ft, sw, sb, mw, mb)


def on_device(source, routes, slot_weights, window, stem_weight, stem_bias, mix_weight, mix_bias):
    band = lax.axis_index("band")
    flags = jnp.stack([band == 0, band == lax.axis_size("band") - 1]).astype(jnp.int32)
    windows = gather(source, routes, window.reshape(1, 384), slot_weights.reshape(12, 4096, 128))
    return conv(
        flags,
        windows,
        stem_weight.reshape(72, 128),
        stem_bias.reshape(1, 128),
        mix_weight,
        mix_bias.reshape(1, 128),
    )


def solution(mesh):
    in_specs = (
        P(("band", "lon"), None, None),
        P(("band", "lon"), None),
        P(("band", "lon"), None, None, None, None),
        P(("band", "lon"), None, None),
        P(),
        P(),
        P(),
        P(),
    )
    out_specs = P("band", "lon", None)
    return jax.shard_map(
        on_device, mesh=mesh, in_specs=in_specs, out_specs=out_specs, check_vma=False
    )
```

```python
import jax
import jax.numpy as jnp
from jax import lax
from jax.experimental import pallas as pl
from jax.experimental.pallas import tpu as pltpu
from jax.sharding import PartitionSpec as P

NT = (((1,), (1,)), ((), ()))


def gather_kernel(src, routes, window, weights, out, wv, s32, o32, sendb, recvb, c32, place, fs32, fe, colr, coll,
                  lc, ln, ls, rc, rn, rs, y32, lv, w_sem, send_sem, recv_sem, hs_sem, hr_sem, o_sem, e_sem):
    f32, bf16 = jnp.float32, jnp.bfloat16
    n_band, n_lon = lax.axis_size("band"), lax.axis_size("lon")
    band, lon = lax.axis_index("band"), lax.axis_index("lon")
    barrier = pltpu.get_barrier_semaphore()

    def there(q):
        return {"band": band + (q // 4 - 1), "lon": lax.rem(lon + q % 4, n_lon)}

    def inside(b):
        return jnp.logical_and(b >= 0, b < n_band)

    def edge(b):
        return jnp.logical_or(b == 0, b == n_band - 1)

    def sends(q):
        ok = inside(band + (q // 4 - 1))
        return jnp.logical_and(ok, edge(band)) if q % 4 == 2 else ok

    def gets(q):
        origin = band - (q // 4 - 1)
        return jnp.logical_and(inside(origin), edge(origin)) if q % 4 == 2 else inside(origin)

    def greets(q):
        target = band + (q // 4 - 1)
        ok = inside(target)
        return jnp.logical_and(ok, jnp.logical_or(edge(band), edge(target))) if q % 4 == 2 else ok

    others = [q for q in range(12) if q != 4]
    count = jnp.int32(0)
    for q in others:
        @pl.when(greets(q))
        def _():
            pl.semaphore_signal(barrier, inc=1, device_id=there(q), device_id_type=pl.DeviceIdType.MESH)
        count = count + greets(q).astype(jnp.int32)

    order = (4, 0, 8, 5, 7, 1, 3, 9, 11, 6, 2, 10)

    def fetch(q):
        return pltpu.make_async_copy(weights.at[q], wv.at[q], w_sem.at[q])

    for q in order:
        fetch(q).start()

    code = lax.broadcasted_iota(jnp.int32, (16, 128), 0)
    names = jnp.logical_or(routes[0:1, :] == code, routes[1:2, :] == code)
    earlier = lax.broadcasted_iota(jnp.int32, (128, 128), 0) < lax.broadcasted_iota(jnp.int32, (128, 128), 1)
    rank = jnp.dot(
        names.astype(f32).astype(bf16), earlier.astype(f32).astype(bf16), preferred_element_type=f32
    )
    ranked = jnp.where(names, rank, -1.0)
    slot = lax.broadcasted_iota(jnp.int32, (32, 128), 0).astype(f32)
    select = jnp.concatenate(
        [(jnp.broadcast_to(ranked[q : q + 1], (32, 128)) == slot).astype(f32) for q in range(12)], axis=0
    ).astype(bf16)
    s32[...] = src[...].astype(f32).reshape(1024, 128)
    for f in range(0, 8, 2):
        planes = jnp.concatenate(
            [s32[pl.ds(f + i, 128, stride=8), :].astype(bf16) for i in range(2)], axis=1
        )
        packed = jnp.dot(select, planes, preferred_element_type=f32)
        for i in range(2):
            o32[pl.ds(f + i, 384, stride=8), :] = packed[:, i * 128 : i * 128 + 128]
    for q in range(12):
        sendb[q] = o32[q * 256 : q * 256 + 256, :].astype(bf16)

    pl.semaphore_wait(barrier, count)

    def route(q):
        return pltpu.make_async_remote_copy(
            src_ref=sendb.at[q], dst_ref=recvb.at[q], send_sem=send_sem.at[q], recv_sem=recv_sem.at[q],
            device_id=there(q), device_id_type=pl.DeviceIdType.MESH,
        )

    for q in (2, 6, 10, 1, 3, 9, 11, 5, 7, 0, 8):
        @pl.when(sends(q))
        def _():
            route(q).start()

    spot = lax.broadcasted_iota(jnp.int32, (256, 384), 0)
    wanted = lax.rem(spot, 64) * 4 + lax.div(spot, 64)
    lands = jnp.concatenate([window[q] for q in range(12)], axis=1)
    place[...] = (jnp.broadcast_to(lands, (256, 384)) == wanted).astype(f32).astype(bf16)
    zero_rows = jnp.zeros((16, 512), bf16)
    zero_tile = jnp.zeros((16, 128), bf16)
    fe[544:592, :] = jnp.zeros((48, 512), bf16)

    @pl.when(band == 0)
    def _():
        fe[0:16, :] = zero_rows
        ln[...] = zero_tile
        rn[...] = zero_tile

    @pl.when(band == n_band - 1)
    def _():
        fe[528:544, :] = zero_rows
        ls[...] = zero_tile
        rs[...] = zero_tile

    for q in order:
        if q == 4:
            held = sendb.at[4]
        else:
            held = recvb.at[q]

            @pl.when(gets(q))
            def _():
                route(q).wait_recv()

            @pl.when(jnp.logical_not(gets(q)))
            def _():
                recvb[q] = jnp.zeros((256, 128), bf16)

        fetch(q).wait()

        for i in range(16):
            col = i * 256
            both = jnp.concatenate([wv[q, col : col + 128, :], wv[q, col + 128 : col + 256, :]], axis=1)
            got = jnp.dot(held[i * 16 : i * 16 + 16, :], both, preferred_element_type=f32)
            c32[q * 256 + i * 16 : q * 256 + i * 16 + 8, :] = got[0:8, 0:128]
            c32[q * 256 + i * 16 + 8 : q * 256 + i * 16 + 16, :] = got[8:16, 128:256]

    for f in range(0, 8, 2):
        planes = jnp.concatenate(
            [c32[pl.ds(f + i, 384, stride=8), :].astype(bf16) for i in range(2)], axis=1
        )
        summed = jnp.dot(place[...], planes, preferred_element_type=f32)
        for i in range(2):
            for c in range(4):
                fs32[c, pl.ds(f + i, 64, stride=8), :] = summed[
                    c * 64 : c * 64 + 64, i * 128 : i * 128 + 128
                ]
    for c in range(4):
        fe[16:528, c * 128 : c * 128 + 128] = fs32[c].astype(bf16)

    pick_row = lax.broadcasted_iota(jnp.int32, (16, 128), 0)
    pick_col = lax.broadcasted_iota(jnp.int32, (16, 128), 1)
    pick_left = jnp.logical_and(pick_row == pick_col, pick_row < 2).astype(f32).astype(bf16)
    pick_right = (pick_col == pick_row + 112).astype(f32)
    pick_right = jnp.where(pick_row >= 14, pick_right, 0.0).astype(bf16)
    coll[...] = lax.dot_general(pick_left, fe[16:528, 0:128], NT, preferred_element_type=f32).astype(bf16)
    colr[...] = lax.dot_general(pick_right, fe[16:528, 384:512], NT, preferred_element_type=f32).astype(bf16)

    east, west = lax.rem(lon + 1, n_lon), lax.rem(lon + n_lon - 1, n_lon)
    north, south = band - 1, band + 1

    def halo(i, source, target, b, l):
        return pltpu.make_async_remote_copy(
            src_ref=source, dst_ref=target, send_sem=hs_sem.at[i], recv_sem=hr_sem.at[i],
            device_id={"band": b, "lon": l}, device_id_type=pl.DeviceIdType.MESH,
        )

    up = [
        halo(0, colr.at[:, 0:128], ls, north, east),
        halo(1, coll.at[:, 0:128], rs, north, west),
        halo(2, fe.at[16:32, :], fe.at[528:544, :], north, lon),
    ]
    down = [
        halo(3, colr.at[:, 384:512], ln, south, east),
        halo(4, coll.at[:, 384:512], rn, south, west),
        halo(5, fe.at[512:528, :], fe.at[0:16, :], south, lon),
    ]
    side = [halo(6, colr, lc, band, east), halo(7, coll, rc, band, west)]

    @pl.when(band > 0)
    def _():
        for c in up:
            c.start()

    @pl.when(band < n_band - 1)
    def _():
        for c in down:
            c.start()

    for c in side:
        c.start()

    same = (lax.broadcasted_iota(jnp.int32, (128, 128), 0) == lax.broadcasted_iota(jnp.int32, (128, 128), 1))
    same = same.astype(f32).astype(bf16)
    pad = jnp.zeros((16, 128), bf16)

    def turn(w):
        for t in range(4):
            piece = fe[64 * w : 64 * w + 80, t * 128 : t * 128 + 128]
            turned = lax.dot_general(
                same, jnp.concatenate([piece, piece, piece, pad], axis=0), NT, preferred_element_type=f32
            )
            for i in range(2):
                y32[w, i, 16 + t * 128 : 144 + t * 128, :] = turned[:, i * 128 : i * 128 + 128]

    def shift(w, start, size):
        lane = lax.broadcasted_iota(jnp.int32, (size, 128), 1)
        at = [slice(start + 14 + b, start + 14 + b + size) for b in range(3)]
        low = jnp.where(lane < 80, y32[w, 0, at[0], :], y32[w, 0, at[1], :])
        high = jnp.where(lane < 32, y32[w, 1, at[1], :], y32[w, 1, at[2], :])
        lv[w, start : start + size, 0:128] = low.astype(bf16)
        lv[w, start : start + size, 128:256] = high.astype(bf16)

    def body_out(w):
        return pltpu.make_async_copy(lv.at[w, 16:496, :], out.at[w, 16:496, :], o_sem.at[w])

    def ends_out(i):
        part = (slice(0, 16), slice(496, 528))[i]
        return pltpu.make_async_copy(lv.at[:, part, :], out.at[:, part, :], e_sem.at[i])

    for w in range(1, 8):
        turn(w)
        shift(w, 16, 480)
        body_out(w).start()

    @pl.when(band < n_band - 1)
    def _():
        for c in up:
            c.wait_recv()

    @pl.when(band > 0)
    def _():
        for c in down:
            c.wait_recv()

    for c in side:
        c.wait_recv()
    for w in (0, 8):
        turn(w)
        shift(w, 16, 480)
        body_out(w).start()

    lane = lax.broadcasted_iota(jnp.int32, (16, 640), 1)
    blank = jnp.zeros((16, 512), f32)
    mid = lc[...].astype(f32) + rc[...].astype(f32)
    mid = pltpu.roll(jnp.concatenate([mid, jnp.zeros((16, 128), f32)], axis=1), 16, 1)
    top = jnp.concatenate([pltpu.roll(ln[...].astype(f32) + rn[...].astype(f32), 16, 1), blank], axis=1)
    low = jnp.concatenate([blank, pltpu.roll(ls[...].astype(f32) + rs[...].astype(f32), 16, 1)], axis=1)
    whole = jnp.where(lane < 16, top, jnp.where(lane < 528, mid, jnp.where(lane < 544, low, 0.0)))
    lane = lax.broadcasted_iota(jnp.int32, (16, 256), 1)
    for w in range(9):
        first = (whole if w == 0 else pltpu.roll(whole, 640 - 64 * w, 1))[:, 0:256]
        first = jnp.where(lane < 80, first, 0.0)
        first = first + pltpu.roll(first, 80, 1) + pltpu.roll(first, 160, 1)
        for i in range(2):
            y32[w, i, 0:16, :] = first[:, i * 128 : i * 128 + 128]
            y32[w, i, 528:544, :] = first[:, i * 128 : i * 128 + 128]
        shift(w, 0, 16)
        shift(w, 496, 32)
    for i in range(2):
        ends_out(i).start()
    for w in range(9):
        body_out(w).wait()
    for i in range(2):
        ends_out(i).wait()

    for q in others:
        @pl.when(sends(q))
        def _():
            route(q).wait_send()

    @pl.when(band > 0)
    def _():
        for c in up:
            c.wait_send()

    @pl.when(band < n_band - 1)
    def _():
        for c in down:
            c.wait_send()

    for c in side:
        c.wait_send()


def gather(source, routes, window, weights):
    V, D = pltpu.VMEM, pltpu.SemaphoreType.DMA
    bf16, f32 = jnp.bfloat16, jnp.float32
    vm = pl.BlockSpec(memory_space=pltpu.VMEM)
    return pl.pallas_call(
        gather_kernel,
        out_shape=jax.ShapeDtypeStruct((9, 528, 256), bf16),
        in_specs=[vm, vm, vm, pl.BlockSpec(memory_space=pl.ANY)],
        out_specs=pl.BlockSpec(memory_space=pl.ANY),
        scratch_shapes=[
            V((12, 4096, 128), bf16), V((1024, 128), f32), V((3072, 128), f32),
            V((12, 256, 128), bf16), V((12, 256, 128), bf16), V((3072, 128), f32),
            V((256, 384), bf16), V((4, 512, 128), f32), V((592, 512), bf16),
            V((16, 512), bf16), V((16, 512), bf16),
            V((16, 512), bf16), V((16, 128), bf16), V((16, 128), bf16),
            V((16, 512), bf16), V((16, 128), bf16), V((16, 128), bf16),
            V((9, 2, 544, 128), f32), V((9, 528, 256), bf16),
            D((12,)), D((12,)), D((12,)), D((8,)), D((8,)), D((9,)), D((2,)),
        ],
        compiler_params=pltpu.CompilerParams(
            collective_id=0, has_side_effects=True, vmem_limit_bytes=56 * 1024 * 1024
        ),
        name="gather",
    )(source, routes, window, weights)


UNROLL = 4

def conv_kernel(lhs, sw, sb, mw, mb, out, tmat, ma, ml, mr, lv, h32, r0, r1, r2, r3, h32b, y32, y32b, o0, o1, o2, o3, lsem, sems):
    f32, bf16 = jnp.float32, jnp.bfloat16
    band, n_band = lax.axis_index("band"), lax.axis_size("band")

    def load(w):
        return pltpu.make_async_copy(lhs.at[w], lv.at[w], lsem.at[w])

    for w in range(9):
        load(w).start()

    sw32 = sw[...].astype(f32)
    for j in range(4):
        for y in range(2):
            top = 2 * j + y
            pieces = []
            for b in range(3):
                if top > 0:
                    pieces.append(jnp.zeros((8 * top, 128), f32))
                for a in range(3):
                    pieces.append(sw32[(3 * a + b) * 8 : (3 * a + b) * 8 + 8])
                if top < 7:
                    pieces.append(jnp.zeros((8 * (7 - top), 128), f32))
            pieces.append(jnp.zeros((16, 128), f32))
            tmat[j, :, y * 128 : y * 128 + 128] = jnp.concatenate(pieces, axis=0).astype(bf16)
    for a in range(3):
        row = a * 256
        ma[row : row + 128, 0:128] = mw[3 * a + 1]
        ma[row : row + 128, 128:256] = mw[3 * a]
        ma[row + 128 : row + 256, 0:128] = mw[3 * a + 2]
        ma[row + 128 : row + 256, 128:256] = mw[3 * a + 1]
    for side, b in ((ml, 0), (mr, 2)):
        for r in range(4):
            for o in range(2):
                a = r - o
                block = mw[3 * a + b] if 0 <= a <= 2 else jnp.zeros((128, 128), bf16)
                side[r * 128 : r * 128 + 128, o * 128 : o * 128 + 128] = block

    hb = sb[...] * 0.5
    bias = mb[...]

    def stem(pair, ring, h32):
        w = pair // 4
        acc = jnp.dot(lv[w, 0:520], tmat[pair - w * 4], preferred_element_type=f32)
        for y in range(2):
            u = acc[:, y * 128 : y * 128 + 128] * 0.5 + hb
            h = u + u * jnp.tanh(u)
            row = 2 * pair + y
            gone = jnp.logical_or(
                jnp.logical_and(band == 0, row == 0), jnp.logical_and(band == n_band - 1, row == 65)
            )
            h32[y] = h * jnp.where(gone, 0.0, 1.0)
            for i, start in enumerate((1, 2, 0, 3)):
                ring[y, :, i * 128 : i * 128 + 128] = h32[y, pl.ds(start, 256, stride=2), :].astype(bf16)

    def mix(lo, hi, ob, y32):
        rows = (lo.at[0], lo.at[1], hi.at[0], hi.at[1])
        left = jnp.dot(
            jnp.concatenate([r[:, 256:384] for r in rows], axis=1), ml[...], preferred_element_type=f32
        )
        right = jnp.dot(
            jnp.concatenate([r[:, 384:512] for r in rows], axis=1), mr[...], preferred_element_type=f32
        )
        for o in range(2):
            both = jnp.dot(
                jnp.concatenate([r[:, 0:256] for r in rows[o : o + 3]], axis=1), ma[...], preferred_element_type=f32
            )
            cut = slice(o * 128, o * 128 + 128)
            y32[o, pl.ds(0, 256, stride=2), :] = both[:, 0:128] + left[:, cut] + bias
            y32[o, pl.ds(1, 256, stride=2), :] = both[:, 128:256] + right[:, cut] + bias
            ob[o] = y32[o].astype(bf16)

    rings = (r0, r1, r2, r3)
    obs = (o0, o1, o2, o3)
    hs = (h32, h32b)
    ys = (y32, y32b)
    load(0).wait()
    for pair in range(3):
        stem(jnp.int32(pair), rings[pair], hs[pair % 2])
    for w in range(1, 9):
        load(w).wait()

    def put(p, i):
        return pltpu.make_async_copy(obs[i], out.at[pl.ds(2 * p, 2)], sems.at[i])

    def body(t, carry):
        for i in range(UNROLL):
            p = UNROLL * t + i
            if i < 4:
                @pl.when(t > 0)
                def _():
                    put(p - 4, i % 4).wait()
            else:
                put(p - 4, i % 4).wait()
            stem(p + 3, rings[(i + 3) % 4], hs[(i + 1) % 2])
            mix(rings[i % 4], rings[(i + 1) % 4], obs[i % 4], ys[i % 2])
            put(p, i % 4).start()
        return carry

    lax.fori_loop(0, 32 // UNROLL, body, 0)
    for i in range(4):
        put(28 + i, i).wait()


def conv(lhs, sw, sb, mw, mb):
    V = pltpu.VMEM
    bf16, f32 = jnp.bfloat16, jnp.float32
    vm = pl.BlockSpec(memory_space=pltpu.VMEM)
    return pl.pallas_call(
        conv_kernel,
        out_shape=jax.ShapeDtypeStruct((64, 512, 128), bf16),
        in_specs=[pl.BlockSpec(memory_space=pl.ANY)] + [vm] * 4,
        out_specs=pl.BlockSpec(memory_space=pl.ANY),
        scratch_shapes=[
            V((4, 256, 256), bf16), V((768, 256), bf16), V((512, 256), bf16), V((512, 256), bf16),
            V((9, 528, 256), bf16), V((2, 520, 128), f32),
            V((2, 256, 512), bf16), V((2, 256, 512), bf16), V((2, 256, 512), bf16), V((2, 256, 512), bf16),
            V((2, 520, 128), f32), V((2, 512, 128), f32), V((2, 512, 128), f32),
            V((2, 512, 128), bf16), V((2, 512, 128), bf16), V((2, 512, 128), bf16), V((2, 512, 128), bf16),
            pltpu.SemaphoreType.DMA((9,)), pltpu.SemaphoreType.DMA((4,)),
        ],
        compiler_params=pltpu.CompilerParams(vmem_limit_bytes=56 * 1024 * 1024),
        name="conv",
    )(lhs, sw, sb, mw, mb)


def on_device(source, routes, slot_weights, window, stem_weight, stem_bias, mix_weight, mix_bias):
    columns = gather(source, routes.T, window.transpose(1, 0, 2), slot_weights.reshape(12, 4096, 128))
    return conv(
        columns,
        stem_weight.reshape(72, 128),
        stem_bias.reshape(1, 128),
        mix_weight,
        mix_bias.reshape(1, 128),
    )


def solution(mesh):
    in_specs = (
        P(("band", "lon"), None, None),
        P(("band", "lon"), None),
        P(("band", "lon"), None, None, None, None),
        P(("band", "lon"), None, None),
        P(),
        P(),
        P(),
        P(),
    )
    out_specs = P("band", "lon", None)
    return jax.shard_map(
        on_device, mesh=mesh, in_specs=in_specs, out_specs=out_specs, check_vma=False
    )
```

```python
import jax
import jax.numpy as jnp
from jax import lax
from jax.experimental import pallas as pl
from jax.experimental.pallas import tpu as pltpu
from jax.sharding import PartitionSpec as P

NT = (((1,), (1,)), ((), ()))


def gather_kernel(src_hbm, routes_hbm, window_hbm, weights, out, src, routes, window, wv, s32, o32, sendb, recvb, c32, place, fs32, fe, colr, coll,
                  lc, ln, ls, rc, rn, rs, y32, lv, w_sem, send_sem, recv_sem, hs_sem, hr_sem, o_sem, e_sem, i_sem):
    f32, bf16 = jnp.float32, jnp.bfloat16
    n_band, n_lon = lax.axis_size("band"), lax.axis_size("lon")
    band, lon = lax.axis_index("band"), lax.axis_index("lon")
    barrier = pltpu.get_barrier_semaphore()

    def there(q):
        return {"band": band + (q // 4 - 1), "lon": lax.rem(lon + q % 4, n_lon)}

    def inside(b):
        return jnp.logical_and(b >= 0, b < n_band)

    def edge(b):
        return jnp.logical_or(b == 0, b == n_band - 1)

    def sends(q):
        ok = inside(band + (q // 4 - 1))
        return jnp.logical_and(ok, edge(band)) if q % 4 == 2 else ok

    def gets(q):
        origin = band - (q // 4 - 1)
        return jnp.logical_and(inside(origin), edge(origin)) if q % 4 == 2 else inside(origin)

    def greets(q):
        target = band + (q // 4 - 1)
        ok = inside(target)
        return jnp.logical_and(ok, jnp.logical_or(edge(band), edge(target))) if q % 4 == 2 else ok

    inputs = [
        pltpu.make_async_copy(source, target, i_sem.at[i])
        for i, (source, target) in enumerate(((src_hbm, src), (routes_hbm, routes), (window_hbm, window)))
    ]
    for c in inputs:
        c.start()
    others = [q for q in range(12) if q != 4]
    count = jnp.int32(0)
    for q in others:
        @pl.when(greets(q))
        def _():
            pl.semaphore_signal(barrier, inc=1, device_id=there(q), device_id_type=pl.DeviceIdType.MESH)
        count = count + greets(q).astype(jnp.int32)

    order = (4, 0, 8, 1, 3, 9, 11, 5, 7, 2, 10, 6)

    def fetch(q):
        return pltpu.make_async_copy(weights.at[q], wv.at[q], w_sem.at[q])

    for q in order:
        fetch(q).start()

    inputs[1].wait()
    code = lax.broadcasted_iota(jnp.int32, (16, 128), 0)
    names = jnp.logical_or(routes[0:1, :] == code, routes[1:2, :] == code)
    earlier = lax.broadcasted_iota(jnp.int32, (128, 128), 0) < lax.broadcasted_iota(jnp.int32, (128, 128), 1)
    rank = jnp.dot(
        names.astype(f32).astype(bf16), earlier.astype(f32).astype(bf16), preferred_element_type=f32
    )
    ranked = jnp.where(names, rank, -1.0)
    slot = lax.broadcasted_iota(jnp.int32, (32, 128), 0).astype(f32)
    select = jnp.concatenate(
        [(jnp.broadcast_to(ranked[q : q + 1], (32, 128)) == slot).astype(f32) for q in range(12)], axis=0
    ).astype(bf16)
    inputs[0].wait()
    s32[...] = src[...].astype(f32).reshape(1024, 128)
    for f in range(0, 8, 2):
        planes = jnp.concatenate(
            [s32[pl.ds(f + i, 128, stride=8), :].astype(bf16) for i in range(2)], axis=1
        )
        packed = jnp.dot(select, planes, preferred_element_type=f32)
        for i in range(2):
            o32[pl.ds(f + i, 384, stride=8), :] = packed[:, i * 128 : i * 128 + 128]
    for q in range(12):
        sendb[q] = o32[q * 256 : q * 256 + 256, :].astype(bf16)

    pl.semaphore_wait(barrier, count)

    def route(q):
        return pltpu.make_async_remote_copy(
            src_ref=sendb.at[q], dst_ref=recvb.at[q], send_sem=send_sem.at[q], recv_sem=recv_sem.at[q],
            device_id=there(q), device_id_type=pl.DeviceIdType.MESH,
        )

    for q in (2, 6, 10, 1, 3, 0, 8, 9, 11, 5, 7):
        @pl.when(sends(q))
        def _():
            route(q).start()

    spot = lax.broadcasted_iota(jnp.int32, (256, 384), 0)
    wanted = lax.rem(spot, 64) * 4 + lax.div(spot, 64)
    inputs[2].wait()
    lands = jnp.concatenate([window[q] for q in range(12)], axis=1)
    place[...] = (jnp.broadcast_to(lands, (256, 384)) == wanted).astype(f32).astype(bf16)
    zero_rows = jnp.zeros((16, 512), bf16)
    zero_tile = jnp.zeros((16, 128), bf16)
    fe[544:592, :] = jnp.zeros((48, 512), bf16)

    @pl.when(band == 0)
    def _():
        fe[0:16, :] = zero_rows
        ln[...] = zero_tile
        rn[...] = zero_tile

    @pl.when(band == n_band - 1)
    def _():
        fe[528:544, :] = zero_rows
        ls[...] = zero_tile
        rs[...] = zero_tile

    for q in order:
        if q == 4:
            held = sendb.at[4]
        else:
            held = recvb.at[q]

            @pl.when(gets(q))
            def _():
                route(q).wait_recv()

            @pl.when(jnp.logical_not(gets(q)))
            def _():
                recvb[q] = jnp.zeros((256, 128), bf16)

        fetch(q).wait()

        for i in range(16):
            col = i * 256
            both = jnp.concatenate([wv[q, col : col + 128, :], wv[q, col + 128 : col + 256, :]], axis=1)
            got = jnp.dot(held[i * 16 : i * 16 + 16, :], both, preferred_element_type=f32)
            c32[q * 256 + i * 16 : q * 256 + i * 16 + 8, :] = got[0:8, 0:128]
            c32[q * 256 + i * 16 + 8 : q * 256 + i * 16 + 16, :] = got[8:16, 128:256]

    for f in range(0, 8, 2):
        planes = jnp.concatenate(
            [c32[pl.ds(f + i, 384, stride=8), :].astype(bf16) for i in range(2)], axis=1
        )
        summed = jnp.dot(place[...], planes, preferred_element_type=f32)
        for i in range(2):
            for c in range(4):
                fs32[c, pl.ds(f + i, 64, stride=8), :] = summed[
                    c * 64 : c * 64 + 64, i * 128 : i * 128 + 128
                ]
    for c in range(4):
        fe[16:528, c * 128 : c * 128 + 128] = fs32[c].astype(bf16)

    pick_row = lax.broadcasted_iota(jnp.int32, (16, 128), 0)
    pick_col = lax.broadcasted_iota(jnp.int32, (16, 128), 1)
    pick_left = jnp.logical_and(pick_row == pick_col, pick_row < 2).astype(f32).astype(bf16)
    pick_right = (pick_col == pick_row + 112).astype(f32)
    pick_right = jnp.where(pick_row >= 14, pick_right, 0.0).astype(bf16)
    coll[...] = lax.dot_general(pick_left, fe[16:528, 0:128], NT, preferred_element_type=f32).astype(bf16)
    colr[...] = lax.dot_general(pick_right, fe[16:528, 384:512], NT, preferred_element_type=f32).astype(bf16)

    east, west = lax.rem(lon + 1, n_lon), lax.rem(lon + n_lon - 1, n_lon)
    north, south = band - 1, band + 1

    def halo(i, source, target, b, l):
        return pltpu.make_async_remote_copy(
            src_ref=source, dst_ref=target, send_sem=hs_sem.at[i], recv_sem=hr_sem.at[i],
            device_id={"band": b, "lon": l}, device_id_type=pl.DeviceIdType.MESH,
        )

    up = [
        halo(0, colr.at[:, 0:128], ls, north, east),
        halo(1, coll.at[:, 0:128], rs, north, west),
        halo(2, fe.at[16:32, :], fe.at[528:544, :], north, lon),
    ]
    down = [
        halo(3, colr.at[:, 384:512], ln, south, east),
        halo(4, coll.at[:, 384:512], rn, south, west),
        halo(5, fe.at[512:528, :], fe.at[0:16, :], south, lon),
    ]
    side = [halo(6, colr, lc, band, east), halo(7, coll, rc, band, west)]

    @pl.when(band > 0)
    def _():
        for c in up:
            c.start()

    @pl.when(band < n_band - 1)
    def _():
        for c in down:
            c.start()

    for c in side:
        c.start()

    same = (lax.broadcasted_iota(jnp.int32, (128, 128), 0) == lax.broadcasted_iota(jnp.int32, (128, 128), 1))
    same = same.astype(f32).astype(bf16)
    pad = jnp.zeros((16, 128), bf16)

    def turn(w):
        for t in range(4):
            piece = fe[64 * w : 64 * w + 80, t * 128 : t * 128 + 128]
            turned = lax.dot_general(
                same, jnp.concatenate([piece, piece, piece, pad], axis=0), NT, preferred_element_type=f32
            )
            for i in range(2):
                y32[w, i, 16 + t * 128 : 144 + t * 128, :] = turned[:, i * 128 : i * 128 + 128]

    def shift(w, start, size):
        lane = lax.broadcasted_iota(jnp.int32, (size, 128), 1)
        at = [slice(start + 14 + b, start + 14 + b + size) for b in range(3)]
        low = jnp.where(lane < 80, y32[w, 0, at[0], :], y32[w, 0, at[1], :])
        high = jnp.where(lane < 32, y32[w, 1, at[1], :], y32[w, 1, at[2], :])
        lv[w, start : start + size, 0:128] = low.astype(bf16)
        lv[w, start : start + size, 128:256] = high.astype(bf16)

    def body_out(w):
        return pltpu.make_async_copy(lv.at[w, 16:496, :], out.at[w, 16:496, :], o_sem.at[w])

    def ends_out(i):
        part = (slice(0, 16), slice(496, 528))[i]
        return pltpu.make_async_copy(lv.at[:, part, :], out.at[:, part, :], e_sem.at[i])

    for w in range(1, 8):
        turn(w)
        shift(w, 16, 480)
        body_out(w).start()

    def arrive(copies):
        for c in copies:
            c.wait_recv()

    @pl.when(band < n_band - 1)
    def _():
        arrive(up[2:])

    @pl.when(band > 0)
    def _():
        arrive(down[2:])

    for w in (0, 8):
        turn(w)
        shift(w, 16, 480)
        body_out(w).start()

    arrive(side)

    @pl.when(band < n_band - 1)
    def _():
        arrive(up[:2])

    @pl.when(band > 0)
    def _():
        arrive(down[:2])

    lane = lax.broadcasted_iota(jnp.int32, (16, 640), 1)
    blank = jnp.zeros((16, 512), f32)
    mid = lc[...].astype(f32) + rc[...].astype(f32)
    mid = pltpu.roll(jnp.concatenate([mid, jnp.zeros((16, 128), f32)], axis=1), 16, 1)
    top = jnp.concatenate([pltpu.roll(ln[...].astype(f32) + rn[...].astype(f32), 16, 1), blank], axis=1)
    low = jnp.concatenate([blank, pltpu.roll(ls[...].astype(f32) + rs[...].astype(f32), 16, 1)], axis=1)
    whole = jnp.where(lane < 16, top, jnp.where(lane < 528, mid, jnp.where(lane < 544, low, 0.0)))
    lane = lax.broadcasted_iota(jnp.int32, (16, 256), 1)
    for w in range(9):
        first = (whole if w == 0 else pltpu.roll(whole, 640 - 64 * w, 1))[:, 0:256]
        first = jnp.where(lane < 80, first, 0.0)
        first = first + pltpu.roll(first, 80, 1) + pltpu.roll(first, 160, 1)
        for i in range(2):
            y32[w, i, 0:16, :] = first[:, i * 128 : i * 128 + 128]
            y32[w, i, 528:544, :] = first[:, i * 128 : i * 128 + 128]
        shift(w, 0, 16)
        shift(w, 496, 32)
    for i in range(2):
        ends_out(i).start()
    for w in range(9):
        body_out(w).wait()
    for i in range(2):
        ends_out(i).wait()

    for q in others:
        @pl.when(sends(q))
        def _():
            route(q).wait_send()

    @pl.when(band > 0)
    def _():
        for c in up:
            c.wait_send()

    @pl.when(band < n_band - 1)
    def _():
        for c in down:
            c.wait_send()

    for c in side:
        c.wait_send()


def gather(source, routes, window, weights):
    V, D = pltpu.VMEM, pltpu.SemaphoreType.DMA
    bf16, f32 = jnp.bfloat16, jnp.float32
    return pl.pallas_call(
        gather_kernel,
        out_shape=jax.ShapeDtypeStruct((9, 528, 256), bf16),
        in_specs=[pl.BlockSpec(memory_space=pl.ANY)] * 4,
        out_specs=pl.BlockSpec(memory_space=pl.ANY),
        scratch_shapes=[
            V((128, 8, 128), bf16), V((2, 128), jnp.int32), V((12, 1, 32), jnp.int32),
            V((12, 4096, 128), bf16), V((1024, 128), f32), V((3072, 128), f32),
            V((12, 256, 128), bf16), V((12, 256, 128), bf16), V((3072, 128), f32),
            V((256, 384), bf16), V((4, 512, 128), f32), V((592, 512), bf16),
            V((16, 512), bf16), V((16, 512), bf16),
            V((16, 512), bf16), V((16, 128), bf16), V((16, 128), bf16),
            V((16, 512), bf16), V((16, 128), bf16), V((16, 128), bf16),
            V((9, 2, 544, 128), f32), V((9, 528, 256), bf16),
            D((12,)), D((12,)), D((12,)), D((8,)), D((8,)), D((9,)), D((2,)), D((3,)),
        ],
        compiler_params=pltpu.CompilerParams(
            collective_id=0, has_side_effects=True, vmem_limit_bytes=56 * 1024 * 1024
        ),
        name="gather",
    )(source, routes, window, weights)


UNROLL = 4
MC = 128
SC = 256

def conv_kernel(lhs, sw, sb, mw, mb, out, tmat, ma, ml, mr, lv, h32, r0, r1, r2, r3, h32b, y32, y32b, o0, o1, o2, o3, lsem, sems):
    f32, bf16 = jnp.float32, jnp.bfloat16
    band, n_band = lax.axis_index("band"), lax.axis_size("band")

    def load(w):
        return pltpu.make_async_copy(lhs.at[w], lv.at[w], lsem.at[w])

    for w in range(9):
        load(w).start()

    sw32 = sw[...].astype(f32)
    for j in range(4):
        for y in range(2):
            top = 2 * j + y
            pieces = []
            for b in range(3):
                if top > 0:
                    pieces.append(jnp.zeros((8 * top, 128), f32))
                for a in range(3):
                    pieces.append(sw32[(3 * a + b) * 8 : (3 * a + b) * 8 + 8])
                if top < 7:
                    pieces.append(jnp.zeros((8 * (7 - top), 128), f32))
            pieces.append(jnp.zeros((16, 128), f32))
            tmat[j, :, y * 128 : y * 128 + 128] = jnp.concatenate(pieces, axis=0).astype(bf16)
    for a in range(3):
        row = a * 256
        ma[row : row + 128, 0:128] = mw[3 * a + 1]
        ma[row : row + 128, 128:256] = mw[3 * a]
        ma[row + 128 : row + 256, 0:128] = mw[3 * a + 2]
        ma[row + 128 : row + 256, 128:256] = mw[3 * a + 1]
    for side, b in ((ml, 0), (mr, 2)):
        for r in range(4):
            for o in range(2):
                a = r - o
                block = mw[3 * a + b] if 0 <= a <= 2 else jnp.zeros((128, 128), bf16)
                side[r * 128 : r * 128 + 128, o * 128 : o * 128 + 128] = block

    hb = sb[...] * 0.5
    bias = mb[...]

    def stem(pair, h32, m, size):
        w = pair // 4
        acc = jnp.dot(lv[w, m : m + size], tmat[pair - w * 4], preferred_element_type=f32)
        for y in range(2):
            u = acc[:, y * 128 : y * 128 + 128] * 0.5 + hb
            h = u + u * jnp.tanh(u)
            row = 2 * pair + y
            gone = jnp.logical_or(
                jnp.logical_and(band == 0, row == 0), jnp.logical_and(band == n_band - 1, row == 65)
            )
            h32[y, m : m + size] = h * jnp.where(gone, 0.0, 1.0)

    def split(ring, h32, m, size):
        for y in range(2):
            for i, start in enumerate((1, 2, 0, 3)):
                ring[y, m : m + size, i * 128 : i * 128 + 128] = h32[
                    y, pl.ds(2 * m + start, size, stride=2), :
                ].astype(bf16)

    def mix(lo, hi, ob, y32, m, size):
        rows = [r[k, m : m + size, :] for r in (lo, hi) for k in range(2)]
        left = jnp.dot(
            jnp.concatenate([r[:, 256:384] for r in rows], axis=1), ml[...], preferred_element_type=f32
        )
        right = jnp.dot(
            jnp.concatenate([r[:, 384:512] for r in rows], axis=1), mr[...], preferred_element_type=f32
        )
        for o in range(2):
            both = jnp.dot(
                jnp.concatenate([r[:, 0:256] for r in rows[o : o + 3]], axis=1), ma[...], preferred_element_type=f32
            )
            cut = slice(o * 128, o * 128 + 128)
            y32[o, pl.ds(2 * m, size, stride=2), :] = both[:, 0:128] + left[:, cut] + bias
            y32[o, pl.ds(2 * m + 1, size, stride=2), :] = both[:, 128:256] + right[:, cut] + bias
            ob[o, 2 * m : 2 * m + 2 * size] = y32[o, 2 * m : 2 * m + 2 * size].astype(bf16)

    def both(stem_args, mix_args):
        cuts = [(k * SC, SC if k < 512 // SC - 1 else SC + 8) for k in range(512 // SC)]
        done = 0
        for k in range(256 // MC):
            if mix_args:
                mix(*mix_args, k * MC, MC)
            if stem_args:
                n = len(cuts) * MC // 256
                for m, size in cuts[k * n : k * n + n]:
                    stem(stem_args[0], stem_args[1], m, size)
        if stem_args:
            for k in range(256 // MC):
                split(stem_args[2], stem_args[1], k * MC, MC)

    rings = (r0, r1, r2, r3)
    obs = (o0, o1, o2, o3)
    hs = (h32, h32b)
    ys = (y32, y32b)
    load(0).wait()
    for pair in range(3):
        both((jnp.int32(pair), hs[pair % 2], rings[pair]), None)
    for w in range(1, 9):
        load(w).wait()

    def put(p, i):
        return pltpu.make_async_copy(obs[i], out.at[pl.ds(2 * p, 2)], sems.at[i])

    def body(t, carry):
        for i in range(UNROLL):
            p = UNROLL * t + i
            if i < 4:
                @pl.when(t > 0)
                def _():
                    put(p - 4, i % 4).wait()
            else:
                put(p - 4, i % 4).wait()
            both((p + 3, hs[(i + 1) % 2], rings[(i + 3) % 4]), (rings[i % 4], rings[(i + 1) % 4], obs[i % 4], ys[i % 2]))
            put(p, i % 4).start()
        return carry

    lax.fori_loop(0, 32 // UNROLL, body, 0)
    for i in range(4):
        put(28 + i, i).wait()


def conv(lhs, sw, sb, mw, mb):
    V = pltpu.VMEM
    bf16, f32 = jnp.bfloat16, jnp.float32
    vm = pl.BlockSpec(memory_space=pltpu.VMEM)
    return pl.pallas_call(
        conv_kernel,
        out_shape=jax.ShapeDtypeStruct((64, 512, 128), bf16),
        in_specs=[pl.BlockSpec(memory_space=pl.ANY)] + [vm] * 4,
        out_specs=pl.BlockSpec(memory_space=pl.ANY),
        scratch_shapes=[
            V((4, 256, 256), bf16), V((768, 256), bf16), V((512, 256), bf16), V((512, 256), bf16),
            V((9, 528, 256), bf16), V((2, 520, 128), f32),
            V((2, 256, 512), bf16), V((2, 256, 512), bf16), V((2, 256, 512), bf16), V((2, 256, 512), bf16),
            V((2, 520, 128), f32), V((2, 512, 128), f32), V((2, 512, 128), f32),
            V((2, 512, 128), bf16), V((2, 512, 128), bf16), V((2, 512, 128), bf16), V((2, 512, 128), bf16),
            pltpu.SemaphoreType.DMA((9,)), pltpu.SemaphoreType.DMA((4,)),
        ],
        compiler_params=pltpu.CompilerParams(vmem_limit_bytes=56 * 1024 * 1024),
        name="conv",
    )(lhs, sw, sb, mw, mb)


def on_device(source, routes, slot_weights, window, stem_weight, stem_bias, mix_weight, mix_bias):
    columns = gather(source, routes.T, window.transpose(1, 0, 2), slot_weights.reshape(12, 4096, 128))
    return conv(
        columns,
        stem_weight.reshape(72, 128),
        stem_bias.reshape(1, 128),
        mix_weight,
        mix_bias.reshape(1, 128),
    )


def solution(mesh):
    in_specs = (
        P(("band", "lon"), None, None),
        P(("band", "lon"), None),
        P(("band", "lon"), None, None, None, None),
        P(("band", "lon"), None, None),
        P(),
        P(),
        P(),
        P(),
    )
    out_specs = P("band", "lon", None)
    return jax.shard_map(
        on_device, mesh=mesh, in_specs=in_specs, out_specs=out_specs, check_vma=False
    )
```

```python
import jax
import jax.numpy as jnp
from jax import lax
from jax.experimental import pallas as pl
from jax.experimental.pallas import tpu as pltpu
from jax.sharding import PartitionSpec as P

NT = (((1,), (1,)), ((), ()))


def gather_kernel(src_hbm, routes_hbm, window_hbm, weights, out, src, routes, window, wv, s32, o32, sendb, recvb, c32, place, fs32, fe, colr, coll,
                  lc, ln, ls, rc, rn, rs, y32, lv, w_sem, send_sem, recv_sem, hs_sem, hr_sem, o_sem, e_sem, i_sem):
    f32, bf16 = jnp.float32, jnp.bfloat16
    n_band, n_lon = lax.axis_size("band"), lax.axis_size("lon")
    band, lon = lax.axis_index("band"), lax.axis_index("lon")
    barrier = pltpu.get_barrier_semaphore()

    def there(q):
        return {"band": band + (q // 4 - 1), "lon": lax.rem(lon + q % 4, n_lon)}

    def inside(b):
        return jnp.logical_and(b >= 0, b < n_band)

    def edge(b):
        return jnp.logical_or(b == 0, b == n_band - 1)

    def sends(q):
        ok = inside(band + (q // 4 - 1))
        return jnp.logical_and(ok, edge(band)) if q % 4 == 2 else ok

    def gets(q):
        origin = band - (q // 4 - 1)
        return jnp.logical_and(inside(origin), edge(origin)) if q % 4 == 2 else inside(origin)

    def greets(q):
        target = band + (q // 4 - 1)
        ok = inside(target)
        return jnp.logical_and(ok, jnp.logical_or(edge(band), edge(target))) if q % 4 == 2 else ok

    inputs = [
        pltpu.make_async_copy(source, target, i_sem.at[i])
        for i, (source, target) in enumerate(((src_hbm, src), (routes_hbm, routes), (window_hbm, window)))
    ]
    for c in inputs:
        c.start()
    others = [q for q in range(12) if q != 4]
    count = jnp.int32(0)
    for q in others:
        @pl.when(greets(q))
        def _():
            pl.semaphore_signal(barrier, inc=1, device_id=there(q), device_id_type=pl.DeviceIdType.MESH)
        count = count + greets(q).astype(jnp.int32)

    order = (4, 0, 8, 2, 6, 10, 1, 3, 9, 11, 5, 7)

    def fetch(q):
        return pltpu.make_async_copy(weights.at[q], wv.at[q], w_sem.at[q])

    fetch(4).start()
    for q in order[1:]:
        @pl.when(gets(q))
        def _():
            fetch(q).start()


    inputs[1].wait()
    code = lax.broadcasted_iota(jnp.int32, (16, 128), 0)
    names = jnp.logical_or(routes[0:1, :] == code, routes[1:2, :] == code)
    earlier = lax.broadcasted_iota(jnp.int32, (128, 128), 0) < lax.broadcasted_iota(jnp.int32, (128, 128), 1)
    rank = jnp.dot(
        names.astype(f32).astype(bf16), earlier.astype(f32).astype(bf16), preferred_element_type=f32
    )
    ranked = jnp.where(names, rank, -1.0)
    slot = lax.broadcasted_iota(jnp.int32, (32, 128), 0).astype(f32)
    select = jnp.concatenate(
        [(jnp.broadcast_to(ranked[q : q + 1], (32, 128)) == slot).astype(f32) for q in range(12)], axis=0
    ).astype(bf16)
    inputs[0].wait()
    s32[...] = src[...].astype(f32).reshape(1024, 128)
    for f in range(0, 8, 2):
        planes = jnp.concatenate(
            [s32[pl.ds(f + i, 128, stride=8), :].astype(bf16) for i in range(2)], axis=1
        )
        packed = jnp.dot(select, planes, preferred_element_type=f32)
        for i in range(2):
            o32[pl.ds(f + i, 384, stride=8), :] = packed[:, i * 128 : i * 128 + 128]
    for q in range(12):
        sendb[q] = o32[q * 256 : q * 256 + 256, :].astype(bf16)

    pl.semaphore_wait(barrier, count)

    def route(q):
        return pltpu.make_async_remote_copy(
            src_ref=sendb.at[q], dst_ref=recvb.at[q], send_sem=send_sem.at[q], recv_sem=recv_sem.at[q],
            device_id=there(q), device_id_type=pl.DeviceIdType.MESH,
        )

    for q in (2, 6, 10, 1, 3, 0, 8, 9, 11, 5, 7):
        @pl.when(sends(q))
        def _():
            route(q).start()

    spot = lax.broadcasted_iota(jnp.int32, (256, 384), 0)
    wanted = lax.rem(spot, 64) * 4 + lax.div(spot, 64)
    inputs[2].wait()
    lands = jnp.concatenate([window[q] for q in range(12)], axis=1)
    place[...] = (jnp.broadcast_to(lands, (256, 384)) == wanted).astype(f32).astype(bf16)
    zero_rows = jnp.zeros((16, 512), bf16)
    zero_tile = jnp.zeros((16, 128), bf16)
    fe[544:592, :] = jnp.zeros((48, 512), bf16)

    @pl.when(band == 0)
    def _():
        fe[0:16, :] = zero_rows
        ln[...] = zero_tile
        rn[...] = zero_tile

    @pl.when(band == n_band - 1)
    def _():
        fe[528:544, :] = zero_rows
        ls[...] = zero_tile
        rs[...] = zero_tile

    def product(q, held):
        fetch(q).wait()
        for i in range(16):
            col = i * 256
            both = jnp.concatenate([wv[q, col : col + 128, :], wv[q, col + 128 : col + 256, :]], axis=1)
            got = jnp.dot(held[i * 16 : i * 16 + 16, :], both, preferred_element_type=f32)
            c32[q * 256 + i * 16 : q * 256 + i * 16 + 8, :] = got[0:8, 0:128]
            c32[q * 256 + i * 16 + 8 : q * 256 + i * 16 + 16, :] = got[8:16, 128:256]

    product(4, sendb.at[4])
    for q in order[1:]:
        @pl.when(gets(q))
        def _():
            route(q).wait_recv()
            product(q, recvb.at[q])

        @pl.when(jnp.logical_not(gets(q)))
        def _():
            c32[q * 256 : q * 256 + 256, :] = jnp.zeros((256, 128), f32)

    for f in range(0, 8, 2):
        planes = jnp.concatenate(
            [c32[pl.ds(f + i, 384, stride=8), :].astype(bf16) for i in range(2)], axis=1
        )
        summed = jnp.dot(place[...], planes, preferred_element_type=f32)
        for i in range(2):
            for c in range(4):
                fs32[c, pl.ds(f + i, 64, stride=8), :] = summed[
                    c * 64 : c * 64 + 64, i * 128 : i * 128 + 128
                ]
    for c in range(4):
        fe[16:528, c * 128 : c * 128 + 128] = fs32[c].astype(bf16)

    pick_row = lax.broadcasted_iota(jnp.int32, (16, 128), 0)
    pick_col = lax.broadcasted_iota(jnp.int32, (16, 128), 1)
    pick_left = jnp.logical_and(pick_row == pick_col, pick_row < 2).astype(f32).astype(bf16)
    pick_right = (pick_col == pick_row + 112).astype(f32)
    pick_right = jnp.where(pick_row >= 14, pick_right, 0.0).astype(bf16)
    coll[...] = lax.dot_general(pick_left, fe[16:528, 0:128], NT, preferred_element_type=f32).astype(bf16)
    colr[...] = lax.dot_general(pick_right, fe[16:528, 384:512], NT, preferred_element_type=f32).astype(bf16)

    east, west = lax.rem(lon + 1, n_lon), lax.rem(lon + n_lon - 1, n_lon)
    north, south = band - 1, band + 1

    def halo(i, source, target, b, l):
        return pltpu.make_async_remote_copy(
            src_ref=source, dst_ref=target, send_sem=hs_sem.at[i], recv_sem=hr_sem.at[i],
            device_id={"band": b, "lon": l}, device_id_type=pl.DeviceIdType.MESH,
        )

    up = [
        halo(0, colr.at[:, 0:128], ls, north, east),
        halo(1, coll.at[:, 0:128], rs, north, west),
        halo(2, fe.at[16:32, :], fe.at[528:544, :], north, lon),
    ]
    down = [
        halo(3, colr.at[:, 384:512], ln, south, east),
        halo(4, coll.at[:, 384:512], rn, south, west),
        halo(5, fe.at[512:528, :], fe.at[0:16, :], south, lon),
    ]
    side = [halo(6, colr, lc, band, east), halo(7, coll, rc, band, west)]

    @pl.when(band > 0)
    def _():
        for c in up:
            c.start()

    @pl.when(band < n_band - 1)
    def _():
        for c in down:
            c.start()

    for c in side:
        c.start()

    same = (lax.broadcasted_iota(jnp.int32, (128, 128), 0) == lax.broadcasted_iota(jnp.int32, (128, 128), 1))
    same = same.astype(f32).astype(bf16)
    pad = jnp.zeros((16, 128), bf16)

    def turn(w):
        for t in range(4):
            piece = fe[64 * w : 64 * w + 80, t * 128 : t * 128 + 128]
            turned = lax.dot_general(
                same, jnp.concatenate([piece, piece, piece, pad], axis=0), NT, preferred_element_type=f32
            )
            for i in range(2):
                y32[w, i, 16 + t * 128 : 144 + t * 128, :] = turned[:, i * 128 : i * 128 + 128]

    def shift(w, start, size):
        lane = lax.broadcasted_iota(jnp.int32, (size, 128), 1)
        at = [slice(start + 14 + b, start + 14 + b + size) for b in range(3)]
        low = jnp.where(lane < 80, y32[w, 0, at[0], :], y32[w, 0, at[1], :])
        high = jnp.where(lane < 32, y32[w, 1, at[1], :], y32[w, 1, at[2], :])
        lv[w, start : start + size, 0:128] = low.astype(bf16)
        lv[w, start : start + size, 128:256] = high.astype(bf16)

    def body_out(w):
        return pltpu.make_async_copy(lv.at[w, 16:496, :], out.at[w, 16:496, :], o_sem.at[w])

    def ends_out(i):
        part = (slice(0, 16), slice(496, 528))[i]
        return pltpu.make_async_copy(lv.at[:, part, :], out.at[:, part, :], e_sem.at[i])

    for w in range(1, 8):
        turn(w)
        shift(w, 16, 480)
        body_out(w).start()

    def arrive(copies):
        for c in copies:
            c.wait_recv()

    @pl.when(band < n_band - 1)
    def _():
        arrive(up[2:])

    @pl.when(band > 0)
    def _():
        arrive(down[2:])

    for w in (0, 8):
        turn(w)
        shift(w, 16, 480)
        body_out(w).start()

    arrive(side)

    @pl.when(band < n_band - 1)
    def _():
        arrive(up[:2])

    @pl.when(band > 0)
    def _():
        arrive(down[:2])

    lane = lax.broadcasted_iota(jnp.int32, (16, 640), 1)
    blank = jnp.zeros((16, 512), f32)
    mid = lc[...].astype(f32) + rc[...].astype(f32)
    mid = pltpu.roll(jnp.concatenate([mid, jnp.zeros((16, 128), f32)], axis=1), 16, 1)
    top = jnp.concatenate([pltpu.roll(ln[...].astype(f32) + rn[...].astype(f32), 16, 1), blank], axis=1)
    low = jnp.concatenate([blank, pltpu.roll(ls[...].astype(f32) + rs[...].astype(f32), 16, 1)], axis=1)
    whole = jnp.where(lane < 16, top, jnp.where(lane < 528, mid, jnp.where(lane < 544, low, 0.0)))
    lane = lax.broadcasted_iota(jnp.int32, (16, 256), 1)
    for w in range(9):
        first = (whole if w == 0 else pltpu.roll(whole, 640 - 64 * w, 1))[:, 0:256]
        first = jnp.where(lane < 80, first, 0.0)
        first = first + pltpu.roll(first, 80, 1) + pltpu.roll(first, 160, 1)
        for i in range(2):
            y32[w, i, 0:16, :] = first[:, i * 128 : i * 128 + 128]
            y32[w, i, 528:544, :] = first[:, i * 128 : i * 128 + 128]
        shift(w, 0, 16)
        shift(w, 496, 32)
    for i in range(2):
        ends_out(i).start()
    for w in range(9):
        body_out(w).wait()
    for i in range(2):
        ends_out(i).wait()

    for q in others:
        @pl.when(sends(q))
        def _():
            route(q).wait_send()

    @pl.when(band > 0)
    def _():
        for c in up:
            c.wait_send()

    @pl.when(band < n_band - 1)
    def _():
        for c in down:
            c.wait_send()

    for c in side:
        c.wait_send()


def gather(source, routes, window, weights):
    V, D = pltpu.VMEM, pltpu.SemaphoreType.DMA
    bf16, f32 = jnp.bfloat16, jnp.float32
    return pl.pallas_call(
        gather_kernel,
        out_shape=jax.ShapeDtypeStruct((9, 528, 256), bf16),
        in_specs=[pl.BlockSpec(memory_space=pltpu.HBM)] * 4,
        out_specs=pl.BlockSpec(memory_space=pl.ANY),
        scratch_shapes=[
            V((128, 8, 128), bf16), V((2, 128), jnp.int32), V((12, 1, 32), jnp.int32),
            V((12, 4096, 128), bf16), V((1024, 128), f32), V((3072, 128), f32),
            V((12, 256, 128), bf16), V((12, 256, 128), bf16), V((3072, 128), f32),
            V((256, 384), bf16), V((4, 512, 128), f32), V((592, 512), bf16),
            V((16, 512), bf16), V((16, 512), bf16),
            V((16, 512), bf16), V((16, 128), bf16), V((16, 128), bf16),
            V((16, 512), bf16), V((16, 128), bf16), V((16, 128), bf16),
            V((9, 2, 544, 128), f32), V((9, 528, 256), bf16),
            D((12,)), D((12,)), D((12,)), D((8,)), D((8,)), D((9,)), D((2,)), D((3,)),
        ],
        compiler_params=pltpu.CompilerParams(
            collective_id=0, has_side_effects=True, vmem_limit_bytes=40 * 1024 * 1024
        ),
        name="gather",
    )(source, routes, window, weights)


UNROLL = 4
MC = 128
SC = 256

def conv_kernel(lhs, sw, sb, mw, mb, out, tmat, ma, ml, mr, lv, h32, r0, r1, r2, r3, h32b, y32, y32b, o0, o1, o2, o3, lsem, sems):
    f32, bf16 = jnp.float32, jnp.bfloat16
    band, n_band = lax.axis_index("band"), lax.axis_size("band")

    def load(w):
        return pltpu.make_async_copy(lhs.at[w], lv.at[w], lsem.at[w])

    for w in range(9):
        load(w).start()

    sw32 = sw[...].astype(f32)
    for j in range(4):
        for y in range(2):
            top = 2 * j + y
            pieces = []
            for b in range(3):
                if top > 0:
                    pieces.append(jnp.zeros((8 * top, 128), f32))
                for a in range(3):
                    pieces.append(sw32[(3 * a + b) * 8 : (3 * a + b) * 8 + 8])
                if top < 7:
                    pieces.append(jnp.zeros((8 * (7 - top), 128), f32))
            pieces.append(jnp.zeros((16, 128), f32))
            tmat[j, :, y * 128 : y * 128 + 128] = jnp.concatenate(pieces, axis=0).astype(bf16)
    for a in range(3):
        row = a * 256
        ma[row : row + 128, 0:128] = mw[3 * a + 1]
        ma[row : row + 128, 128:256] = mw[3 * a]
        ma[row + 128 : row + 256, 0:128] = mw[3 * a + 2]
        ma[row + 128 : row + 256, 128:256] = mw[3 * a + 1]
    for side, b in ((ml, 0), (mr, 2)):
        for r in range(4):
            for o in range(2):
                a = r - o
                block = mw[3 * a + b] if 0 <= a <= 2 else jnp.zeros((128, 128), bf16)
                side[r * 128 : r * 128 + 128, o * 128 : o * 128 + 128] = block

    hb = sb[...] * 0.5
    bias = mb[...]

    def stem(pair, h32, m, size):
        w = pair // 4
        acc = jnp.dot(lv[w, m : m + size], tmat[pair - w * 4], preferred_element_type=f32)
        for y in range(2):
            u = acc[:, y * 128 : y * 128 + 128] * 0.5 + hb
            h = u + u * jnp.tanh(u)
            row = 2 * pair + y
            gone = jnp.logical_or(
                jnp.logical_and(band == 0, row == 0), jnp.logical_and(band == n_band - 1, row == 65)
            )
            h32[y, m : m + size] = h * jnp.where(gone, 0.0, 1.0)

    def split(ring, h32, m, size):
        for y in range(2):
            for i, start in enumerate((1, 2, 0, 3)):
                ring[y, m : m + size, i * 128 : i * 128 + 128] = h32[
                    y, pl.ds(2 * m + start, size, stride=2), :
                ].astype(bf16)

    def mix(lo, hi, ob, y32, m, size):
        rows = [r[k, m : m + size, :] for r in (lo, hi) for k in range(2)]
        left = jnp.dot(
            jnp.concatenate([r[:, 256:384] for r in rows], axis=1), ml[...], preferred_element_type=f32
        )
        right = jnp.dot(
            jnp.concatenate([r[:, 384:512] for r in rows], axis=1), mr[...], preferred_element_type=f32
        )
        for o in range(2):
            both = jnp.dot(
                jnp.concatenate([r[:, 0:256] for r in rows[o : o + 3]], axis=1), ma[...], preferred_element_type=f32
            )
            cut = slice(o * 128, o * 128 + 128)
            y32[o, pl.ds(2 * m, size, stride=2), :] = both[:, 0:128] + left[:, cut] + bias
            y32[o, pl.ds(2 * m + 1, size, stride=2), :] = both[:, 128:256] + right[:, cut] + bias
            ob[o, 2 * m : 2 * m + 2 * size] = y32[o, 2 * m : 2 * m + 2 * size].astype(bf16)

    def both(stem_args, mix_args):
        cuts = [(k * SC, SC if k < 512 // SC - 1 else SC + 8) for k in range(512 // SC)]
        done = 0
        for k in range(256 // MC):
            if mix_args:
                mix(*mix_args, k * MC, MC)
            if stem_args:
                n = len(cuts) * MC // 256
                for m, size in cuts[k * n : k * n + n]:
                    stem(stem_args[0], stem_args[1], m, size)
        if stem_args:
            for k in range(256 // MC):
                split(stem_args[2], stem_args[1], k * MC, MC)

    rings = (r0, r1, r2, r3)
    obs = (o0, o1, o2, o3)
    hs = (h32, h32b)
    ys = (y32, y32b)
    load(0).wait()
    for pair in range(3):
        both((jnp.int32(pair), hs[pair % 2], rings[pair]), None)
    for w in range(1, 9):
        load(w).wait()

    def put(p, i):
        return pltpu.make_async_copy(obs[i], out.at[pl.ds(2 * p, 2)], sems.at[i])

    def body(t, carry):
        for i in range(UNROLL):
            p = UNROLL * t + i
            if i < 4:
                @pl.when(t > 0)
                def _():
                    put(p - 4, i % 4).wait()
            else:
                put(p - 4, i % 4).wait()
            both((p + 3, hs[(i + 1) % 2], rings[(i + 3) % 4]), (rings[i % 4], rings[(i + 1) % 4], obs[i % 4], ys[i % 2]))
            put(p, i % 4).start()
        return carry

    lax.fori_loop(0, 32 // UNROLL, body, 0)
    for i in range(4):
        put(28 + i, i).wait()


def conv(lhs, sw, sb, mw, mb):
    V = pltpu.VMEM
    bf16, f32 = jnp.bfloat16, jnp.float32
    vm = pl.BlockSpec(memory_space=pltpu.VMEM)
    return pl.pallas_call(
        conv_kernel,
        out_shape=jax.ShapeDtypeStruct((64, 512, 128), bf16),
        in_specs=[pl.BlockSpec(memory_space=pl.ANY)] + [vm] * 4,
        out_specs=pl.BlockSpec(memory_space=pl.ANY),
        scratch_shapes=[
            V((4, 256, 256), bf16), V((768, 256), bf16), V((512, 256), bf16), V((512, 256), bf16),
            V((9, 528, 256), bf16), V((2, 520, 128), f32),
            V((2, 256, 512), bf16), V((2, 256, 512), bf16), V((2, 256, 512), bf16), V((2, 256, 512), bf16),
            V((2, 520, 128), f32), V((2, 512, 128), f32), V((2, 512, 128), f32),
            V((2, 512, 128), bf16), V((2, 512, 128), bf16), V((2, 512, 128), bf16), V((2, 512, 128), bf16),
            pltpu.SemaphoreType.DMA((9,)), pltpu.SemaphoreType.DMA((4,)),
        ],
        compiler_params=pltpu.CompilerParams(vmem_limit_bytes=24 * 1024 * 1024),
        name="conv",
    )(lhs, sw, sb, mw, mb)


def on_device(source, routes, slot_weights, window, stem_weight, stem_bias, mix_weight, mix_bias):
    operands = (source, routes.T, window.transpose(1, 0, 2), slot_weights.reshape(12, 4096, 128))
    columns = gather(*(pltpu.with_memory_space_constraint(x, pltpu.HBM) for x in operands))
    return conv(
        columns,
        stem_weight.reshape(72, 128),
        stem_bias.reshape(1, 128),
        mix_weight,
        mix_bias.reshape(1, 128),
    )


def solution(mesh):
    in_specs = (
        P(("band", "lon"), None, None),
        P(("band", "lon"), None),
        P(("band", "lon"), None, None, None, None),
        P(("band", "lon"), None, None),
        P(),
        P(),
        P(),
        P(),
    )
    out_specs = P("band", "lon", None)
    return jax.shard_map(
        on_device, mesh=mesh, in_specs=in_specs, out_specs=out_specs, check_vma=False
    )
```

```python
import jax
import jax.numpy as jnp
from jax import lax
from jax.experimental import pallas as pl
from jax.experimental.pallas import tpu as pltpu
from jax.sharding import PartitionSpec as P

NT = (((1,), (1,)), ((), ()))


def gather_kernel(src_hbm, routes_hbm, window_hbm, weights, out, src, routes, window, wv, s32, o32, sendb, recvb, c32, place, fs32, fe, colr, coll,
                  lc, ln, ls, rc, rn, rs, y32, lv, w_sem, send_sem, recv_sem, hs_sem, hr_sem, o_sem, e_sem, i_sem):
    f32, bf16 = jnp.float32, jnp.bfloat16
    n_band, n_lon = lax.axis_size("band"), lax.axis_size("lon")
    band, lon = lax.axis_index("band"), lax.axis_index("lon")
    barrier = pltpu.get_barrier_semaphore()

    def there(q):
        return {"band": band + (q // 4 - 1), "lon": lax.rem(lon + q % 4, n_lon)}

    def inside(b):
        return jnp.logical_and(b >= 0, b < n_band)

    def edge(b):
        return jnp.logical_or(b == 0, b == n_band - 1)

    def sends(q):
        ok = inside(band + (q // 4 - 1))
        return jnp.logical_and(ok, edge(band)) if q % 4 == 2 else ok

    def gets(q):
        origin = band - (q // 4 - 1)
        return jnp.logical_and(inside(origin), edge(origin)) if q % 4 == 2 else inside(origin)

    def greets(q):
        target = band + (q // 4 - 1)
        ok = inside(target)
        return jnp.logical_and(ok, jnp.logical_or(edge(band), edge(target))) if q % 4 == 2 else ok

    inputs = [
        pltpu.make_async_copy(source, target, i_sem.at[i])
        for i, (source, target) in enumerate(((src_hbm, src), (routes_hbm, routes), (window_hbm, window)))
    ]
    for c in inputs:
        c.start()
    others = (1, 3, 9, 11, 0, 8, 5, 7, 2, 6, 10)
    count = jnp.int32(0)
    for q in others:
        @pl.when(greets(q))
        def _():
            pl.semaphore_signal(barrier, inc=1, device_id=there(q), device_id_type=pl.DeviceIdType.MESH)
        count = count + greets(q).astype(jnp.int32)

    order = (4, 0, 8, 2, 6, 10, 1, 3, 9, 11, 5, 7)

    def fetch(q):
        return pltpu.make_async_copy(weights.at[q], wv.at[q], w_sem.at[q])

    fetch(4).start()
    for q in order[1:]:
        @pl.when(gets(q))
        def _():
            fetch(q).start()


    inputs[1].wait()
    code = lax.broadcasted_iota(jnp.int32, (16, 128), 0)
    names = jnp.logical_or(routes[0:1, :] == code, routes[1:2, :] == code)
    earlier = lax.broadcasted_iota(jnp.int32, (128, 128), 0) < lax.broadcasted_iota(jnp.int32, (128, 128), 1)
    rank = jnp.dot(
        names.astype(f32).astype(bf16), earlier.astype(f32).astype(bf16), preferred_element_type=f32
    )
    ranked = jnp.where(names, rank, -1.0)
    slot = lax.broadcasted_iota(jnp.int32, (32, 128), 0).astype(f32)
    select = jnp.concatenate(
        [(jnp.broadcast_to(ranked[q : q + 1], (32, 128)) == slot).astype(f32) for q in range(12)], axis=0
    ).astype(bf16)
    inputs[0].wait()
    s32[0:1024, :] = src[...].astype(f32).reshape(1024, 128)
    for f in range(0, 8, 2):
        planes = jnp.concatenate(
            [s32[pl.ds(f + i, 128, stride=8), :].astype(bf16) for i in range(2)], axis=1
        )
        packed = jnp.dot(select, planes, preferred_element_type=f32)
        for i in range(2):
            o32[pl.ds(f + i, 384, stride=8), :] = packed[:, i * 128 : i * 128 + 128]
    for q in range(12):
        sendb[q] = o32[q * 256 : q * 256 + 256, :].astype(bf16)

    pl.semaphore_wait(barrier, count)

    def route(q):
        return pltpu.make_async_remote_copy(
            src_ref=sendb.at[q], dst_ref=recvb.at[q], send_sem=send_sem.at[q], recv_sem=recv_sem.at[q],
            device_id=there(q), device_id_type=pl.DeviceIdType.MESH,
        )

    for q in (2, 6, 10, 1, 3, 0, 8, 9, 11, 5, 7):
        @pl.when(sends(q))
        def _():
            route(q).start()

    spot = lax.broadcasted_iota(jnp.int32, (256, 384), 0)
    wanted = lax.rem(spot, 64) * 4 + lax.div(spot, 64)
    inputs[2].wait()
    lands = jnp.concatenate([window[q] for q in range(12)], axis=1)
    place[...] = (jnp.broadcast_to(lands, (256, 384)) == wanted).astype(f32).astype(bf16)
    zero_rows = jnp.zeros((16, 512), bf16)
    zero_tile = jnp.zeros((16, 128), bf16)
    fe[544:592, :] = jnp.zeros((48, 512), bf16)

    @pl.when(band == 0)
    def _():
        fe[0:16, :] = zero_rows
        ln[...] = zero_tile
        rn[...] = zero_tile

    @pl.when(band == n_band - 1)
    def _():
        fe[528:544, :] = zero_rows
        ls[...] = zero_tile
        rs[...] = zero_tile

    def product(q, held):
        fetch(q).wait()
        for i in range(16):
            col = i * 256
            both = jnp.concatenate([wv[q, col : col + 128, :], wv[q, col + 128 : col + 256, :]], axis=1)
            got = jnp.dot(held[i * 16 : i * 16 + 16, :], both, preferred_element_type=f32)
            c32[q * 256 + i * 16 : q * 256 + i * 16 + 8, :] = got[0:8, 0:128]
            c32[q * 256 + i * 16 + 8 : q * 256 + i * 16 + 16, :] = got[8:16, 128:256]

    product(4, sendb.at[4])
    for q in order[1:]:
        @pl.when(gets(q))
        def _():
            route(q).wait_recv()
            product(q, recvb.at[q])

        @pl.when(jnp.logical_not(gets(q)))
        def _():
            c32[q * 256 : q * 256 + 256, :] = jnp.zeros((256, 128), f32)

    for f in range(0, 8, 2):
        planes = jnp.concatenate(
            [c32[pl.ds(f + i, 384, stride=8), :].astype(bf16) for i in range(2)], axis=1
        )
        summed = jnp.dot(place[...], planes, preferred_element_type=f32)
        for i in range(2):
            for c in range(4):
                fs32[c, pl.ds(f + i, 64, stride=8), :] = summed[
                    c * 64 : c * 64 + 64, i * 128 : i * 128 + 128
                ]
    for c in range(4):
        fe[16:528, c * 128 : c * 128 + 128] = fs32[c, 0:512, :].astype(bf16)

    pick_row = lax.broadcasted_iota(jnp.int32, (16, 128), 0)
    pick_col = lax.broadcasted_iota(jnp.int32, (16, 128), 1)
    pick_left = jnp.logical_and(pick_row == pick_col, pick_row < 2).astype(f32).astype(bf16)
    pick_right = (pick_col == pick_row + 112).astype(f32)
    pick_right = jnp.where(pick_row >= 14, pick_right, 0.0).astype(bf16)
    coll[...] = lax.dot_general(pick_left, fe[16:528, 0:128], NT, preferred_element_type=f32).astype(bf16)
    colr[...] = lax.dot_general(pick_right, fe[16:528, 384:512], NT, preferred_element_type=f32).astype(bf16)

    east, west = lax.rem(lon + 1, n_lon), lax.rem(lon + n_lon - 1, n_lon)
    north, south = band - 1, band + 1

    def halo(i, source, target, b, l):
        return pltpu.make_async_remote_copy(
            src_ref=source, dst_ref=target, send_sem=hs_sem.at[i], recv_sem=hr_sem.at[i],
            device_id={"band": b, "lon": l}, device_id_type=pl.DeviceIdType.MESH,
        )

    up = [
        halo(0, colr.at[:, 0:128], ls, north, east),
        halo(1, coll.at[:, 0:128], rs, north, west),
        halo(2, fe.at[16:32, :], fe.at[528:544, :], north, lon),
    ]
    down = [
        halo(3, colr.at[:, 384:512], ln, south, east),
        halo(4, coll.at[:, 384:512], rn, south, west),
        halo(5, fe.at[512:528, :], fe.at[0:16, :], south, lon),
    ]
    side = [halo(6, colr, lc, band, east), halo(7, coll, rc, band, west)]

    @pl.when(band > 0)
    def _():
        for c in up:
            c.start()

    @pl.when(band < n_band - 1)
    def _():
        for c in down:
            c.start()

    for c in side:
        c.start()

    same = (lax.broadcasted_iota(jnp.int32, (128, 128), 0) == lax.broadcasted_iota(jnp.int32, (128, 128), 1))
    same = same.astype(f32).astype(bf16)
    pad = jnp.zeros((16, 128), bf16)

    def turn(w):
        for t in range(4):
            piece = fe[64 * w : 64 * w + 80, t * 128 : t * 128 + 128]
            turned = lax.dot_general(
                same, jnp.concatenate([piece, piece, piece, pad], axis=0), NT, preferred_element_type=f32
            )
            for i in range(2):
                y32[w, i, 16 + t * 128 : 144 + t * 128, :] = turned[:, i * 128 : i * 128 + 128]

    def shift(w, start, size):
        lane = lax.broadcasted_iota(jnp.int32, (size, 128), 1)
        at = [slice(start + 14 + b, start + 14 + b + size) for b in range(3)]
        low = jnp.where(lane < 80, y32[w, 0, at[0], :], y32[w, 0, at[1], :])
        high = jnp.where(lane < 32, y32[w, 1, at[1], :], y32[w, 1, at[2], :])
        lv[w, start : start + size, 0:128] = low.astype(bf16)
        lv[w, start : start + size, 128:256] = high.astype(bf16)

    def body_out(w):
        return pltpu.make_async_copy(lv.at[w, 16:496, :], out.at[w, 16:496, :], o_sem.at[w])

    def ends_out(i):
        part = (slice(0, 16), slice(496, 528))[i % 2]
        group = (slice(1, 8), slice(0, 1), slice(8, 9))[i // 2]
        return pltpu.make_async_copy(lv.at[group, part, :], out.at[group, part, :], e_sem.at[i])

    for w in range(1, 8):
        turn(w)
        shift(w, 16, 480)
        body_out(w).start()

    def arrive(copies):
        for c in copies:
            c.wait_recv()

    @pl.when(band < n_band - 1)
    def _():
        arrive(up[2:])

    @pl.when(band > 0)
    def _():
        arrive(down[2:])

    for w in (0, 8):
        turn(w)
        shift(w, 16, 480)
        body_out(w).start()

    lane = lax.broadcasted_iota(jnp.int32, (16, 640), 1)
    part = lax.broadcasted_iota(jnp.int32, (16, 256), 1)

    def ends(whole, w):
        first = (whole if w == 0 else pltpu.roll(whole, 640 - 64 * w, 1))[:, 0:256]
        first = jnp.where(part < 80, first, 0.0)
        first = first + pltpu.roll(first, 80, 1) + pltpu.roll(first, 160, 1)
        for i in range(2):
            y32[w, i, 0:16, :] = first[:, i * 128 : i * 128 + 128]
            y32[w, i, 528:544, :] = first[:, i * 128 : i * 128 + 128]
        shift(w, 0, 16)
        shift(w, 496, 32)

    arrive(side)
    mid = lc[...].astype(f32) + rc[...].astype(f32)
    mid = pltpu.roll(jnp.concatenate([mid, jnp.zeros((16, 128), f32)], axis=1), 16, 1)
    for w in range(1, 8):
        ends(mid, w)
    for i in range(2):
        ends_out(i).start()

    @pl.when(band < n_band - 1)
    def _():
        arrive(up[:2])

    @pl.when(band > 0)
    def _():
        arrive(down[:2])

    blank = jnp.zeros((16, 512), f32)
    top = jnp.concatenate([pltpu.roll(ln[...].astype(f32) + rn[...].astype(f32), 16, 1), blank], axis=1)
    low = jnp.concatenate([blank, pltpu.roll(ls[...].astype(f32) + rs[...].astype(f32), 16, 1)], axis=1)
    whole = jnp.where(lane < 16, top, jnp.where(lane < 528, mid, jnp.where(lane < 544, low, 0.0)))
    for w in (0, 8):
        ends(whole, w)
    for i in range(2, 6):
        ends_out(i).start()
    for w in range(9):
        body_out(w).wait()
    for i in range(6):
        ends_out(i).wait()

    for q in others:
        @pl.when(sends(q))
        def _():
            route(q).wait_send()

    @pl.when(band > 0)
    def _():
        for c in up:
            c.wait_send()

    @pl.when(band < n_band - 1)
    def _():
        for c in down:
            c.wait_send()

    for c in side:
        c.wait_send()


def gather(source, routes, window, weights):
    V, D = pltpu.VMEM, pltpu.SemaphoreType.DMA
    bf16, f32 = jnp.bfloat16, jnp.float32
    return pl.pallas_call(
        gather_kernel,
        out_shape=jax.ShapeDtypeStruct((9, 528, 256), bf16),
        in_specs=[pl.BlockSpec(memory_space=pltpu.HBM)] * 4,
        out_specs=pl.BlockSpec(memory_space=pl.ANY),
        scratch_shapes=[
            V((128, 8, 128), bf16), V((2, 128), jnp.int32), V((12, 1, 32), jnp.int32),
            V((12, 4096, 128), bf16), V((1032, 128), f32), V((3080, 128), f32),
            V((12, 256, 128), bf16), V((12, 256, 128), bf16), V((3080, 128), f32),
            V((256, 384), bf16), V((4, 520, 128), f32), V((592, 512), bf16),
            V((16, 512), bf16), V((16, 512), bf16),
            V((16, 512), bf16), V((16, 128), bf16), V((16, 128), bf16),
            V((16, 512), bf16), V((16, 128), bf16), V((16, 128), bf16),
            V((9, 2, 544, 128), f32), V((9, 528, 256), bf16),
            D((12,)), D((12,)), D((12,)), D((8,)), D((8,)), D((9,)), D((6,)), D((3,)),
        ],
        compiler_params=pltpu.CompilerParams(
            collective_id=0, has_side_effects=True, vmem_limit_bytes=40 * 1024 * 1024
        ),
        name="gather",
    )(source, routes, window, weights)


UNROLL = 4
MC = 128
SC = 256

def conv_kernel(lv, sw, sb, mw, mb, out, tmat, ma, ml, mr, h32, r0, r1, r2, r3, h32b, y32, y32b, o0, o1, o2, o3, sems):
    f32, bf16 = jnp.float32, jnp.bfloat16
    band, n_band = lax.axis_index("band"), lax.axis_size("band")

    sw32 = sw[...].astype(f32)
    for j in range(4):
        for y in range(2):
            top = 2 * j + y
            pieces = []
            for b in range(3):
                if top > 0:
                    pieces.append(jnp.zeros((8 * top, 128), f32))
                for a in range(3):
                    pieces.append(sw32[(3 * a + b) * 8 : (3 * a + b) * 8 + 8])
                if top < 7:
                    pieces.append(jnp.zeros((8 * (7 - top), 128), f32))
            pieces.append(jnp.zeros((16, 128), f32))
            tmat[j, :, y * 128 : y * 128 + 128] = jnp.concatenate(pieces, axis=0).astype(bf16)
    for a in range(3):
        row = a * 256
        ma[row : row + 128, 0:128] = mw[3 * a + 1]
        ma[row : row + 128, 128:256] = mw[3 * a]
        ma[row + 128 : row + 256, 0:128] = mw[3 * a + 2]
        ma[row + 128 : row + 256, 128:256] = mw[3 * a + 1]
    for side, b in ((ml, 0), (mr, 2)):
        for r in range(4):
            for o in range(2):
                a = r - o
                block = mw[3 * a + b] if 0 <= a <= 2 else jnp.zeros((128, 128), bf16)
                side[r * 128 : r * 128 + 128, o * 128 : o * 128 + 128] = block

    hb = sb[...] * 0.5
    bias = mb[...]

    def stem(pair, h32, m, size):
        w = pair // 4
        acc = jnp.dot(lv[w, m : m + size], tmat[pair - w * 4], preferred_element_type=f32)
        for y in range(2):
            u = acc[:, y * 128 : y * 128 + 128] * 0.5 + hb
            h = u + u * jnp.tanh(u)
            row = 2 * pair + y
            gone = jnp.logical_or(
                jnp.logical_and(band == 0, row == 0), jnp.logical_and(band == n_band - 1, row == 65)
            )
            h32[y, m : m + size] = h * jnp.where(gone, 0.0, 1.0)

    def split(ring, h32, m, size):
        for y in range(2):
            for i, start in enumerate((1, 2, 0, 3)):
                ring[y, m : m + size, i * 128 : i * 128 + 128] = h32[
                    y, pl.ds(2 * m + start, size, stride=2), :
                ].astype(bf16)

    def mix(lo, hi, ob, y32, m, size):
        rows = [r[k, m : m + size, :] for r in (lo, hi) for k in range(2)]
        left = jnp.dot(
            jnp.concatenate([r[:, 256:384] for r in rows], axis=1), ml[...], preferred_element_type=f32
        )
        right = jnp.dot(
            jnp.concatenate([r[:, 384:512] for r in rows], axis=1), mr[...], preferred_element_type=f32
        )
        for o in range(2):
            both = jnp.dot(
                jnp.concatenate([r[:, 0:256] for r in rows[o : o + 3]], axis=1), ma[...], preferred_element_type=f32
            )
            cut = slice(o * 128, o * 128 + 128)
            y32[o, pl.ds(2 * m, size, stride=2), :] = both[:, 0:128] + left[:, cut] + bias
            y32[o, pl.ds(2 * m + 1, size, stride=2), :] = both[:, 128:256] + right[:, cut] + bias
            ob[o, 2 * m : 2 * m + 2 * size] = y32[o, 2 * m : 2 * m + 2 * size].astype(bf16)

    def both(stem_args, mix_args):
        cuts = [(k * SC, SC if k < 512 // SC - 1 else SC + 8) for k in range(512 // SC)]
        done = 0
        for k in range(256 // MC):
            if mix_args:
                mix(*mix_args, k * MC, MC)
            if stem_args:
                n = len(cuts) * MC // 256
                for m, size in cuts[k * n : k * n + n]:
                    stem(stem_args[0], stem_args[1], m, size)
        if stem_args:
            for k in range(256 // MC):
                split(stem_args[2], stem_args[1], k * MC, MC)

    rings = (r0, r1, r2, r3)
    obs = (o0, o1, o2, o3)
    hs = (h32, h32b)
    ys = (y32, y32b)
    for pair in range(3):
        both((jnp.int32(pair), hs[pair % 2], rings[pair]), None)

    def put(p, i):
        return pltpu.make_async_copy(obs[i], out.at[pl.ds(2 * p, 2)], sems.at[i])

    def step(p, i, stems):
        ahead = (p + 3, hs[(i + 1) % 2], rings[(i + 3) % 4]) if stems else None
        both(ahead, (rings[i], rings[(i + 1) % 4], obs[i], ys[i % 2]))
        put(p, i).start()

    def body(t, carry):
        for i in range(4):
            p = 4 * t + i

            @pl.when(t > 0)
            def _():
                put(p - 4, i).wait()

            step(p, i, True)
        return carry

    lax.fori_loop(0, 7, body, 0)
    for i in range(4):
        put(24 + i, i).wait()
        step(jnp.int32(28 + i), i, i < 2)
    for i in range(4):
        put(28 + i, i).wait()


def conv(lhs, sw, sb, mw, mb):
    V = pltpu.VMEM
    bf16, f32 = jnp.bfloat16, jnp.float32
    vm = pl.BlockSpec(memory_space=pltpu.VMEM)
    return pl.pallas_call(
        conv_kernel,
        out_shape=jax.ShapeDtypeStruct((64, 512, 128), bf16),
        in_specs=[vm] * 5,
        out_specs=pl.BlockSpec(memory_space=pl.ANY),
        scratch_shapes=[
            V((4, 256, 256), bf16), V((768, 256), bf16), V((512, 256), bf16), V((512, 256), bf16),
            V((2, 528, 128), f32),
            V((2, 256, 512), bf16), V((2, 256, 512), bf16), V((2, 256, 512), bf16), V((2, 256, 512), bf16),
            V((2, 520, 128), f32), V((2, 520, 128), f32), V((2, 520, 128), f32),
            V((2, 512, 128), bf16), V((2, 512, 128), bf16), V((2, 512, 128), bf16), V((2, 512, 128), bf16),
            pltpu.SemaphoreType.DMA((4,)),
        ],
        compiler_params=pltpu.CompilerParams(vmem_limit_bytes=24 * 1024 * 1024),
        name="conv",
    )(lhs, sw, sb, mw, mb)


def on_device(source, routes, slot_weights, window, stem_weight, stem_bias, mix_weight, mix_bias):
    operands = (source, routes.T, window.transpose(1, 0, 2), slot_weights.reshape(12, 4096, 128))
    columns = gather(*(pltpu.with_memory_space_constraint(x, pltpu.HBM) for x in operands))
    return conv(
        columns,
        stem_weight.reshape(72, 128),
        stem_bias.reshape(1, 128),
        mix_weight,
        mix_bias.reshape(1, 128),
    )


def solution(mesh):
    in_specs = (
        P(("band", "lon"), None, None),
        P(("band", "lon"), None),
        P(("band", "lon"), None, None, None, None),
        P(("band", "lon"), None, None),
        P(),
        P(),
        P(),
        P(),
    )
    out_specs = P("band", "lon", None)
    return jax.shard_map(
        on_device, mesh=mesh, in_specs=in_specs, out_specs=out_specs, check_vma=False
    )
```

```python
import jax
import jax.numpy as jnp
from jax import lax
from jax.experimental import pallas as pl
from jax.experimental.pallas import tpu as pltpu
from jax.sharding import PartitionSpec as P

NT = (((1,), (1,)), ((), ()))


def gather_kernel(src_hbm, routes_hbm, window_hbm, weights, out, src, routes, window, wv, s32, o32, sendb, recvb, c32, place, fs32, fe, colr, coll,
                  lc, ln, ls, rc, rn, rs, y32, lv, w_sem, send_sem, recv_sem, hs_sem, hr_sem, o_sem, e_sem, i_sem):
    f32, bf16 = jnp.float32, jnp.bfloat16
    n_band, n_lon = lax.axis_size("band"), lax.axis_size("lon")
    band, lon = lax.axis_index("band"), lax.axis_index("lon")
    barrier = pltpu.get_barrier_semaphore()

    def there(q):
        return {"band": band + (q // 4 - 1), "lon": lax.rem(lon + q % 4, n_lon)}

    def inside(b):
        return jnp.logical_and(b >= 0, b < n_band)

    def edge(b):
        return jnp.logical_or(b == 0, b == n_band - 1)

    def sends(q):
        ok = inside(band + (q // 4 - 1))
        return jnp.logical_and(ok, edge(band)) if q % 4 == 2 else ok

    def gets(q):
        origin = band - (q // 4 - 1)
        return jnp.logical_and(inside(origin), edge(origin)) if q % 4 == 2 else inside(origin)

    def greets(q):
        target = band + (q // 4 - 1)
        ok = inside(target)
        return jnp.logical_and(ok, jnp.logical_or(edge(band), edge(target))) if q % 4 == 2 else ok

    inputs = [
        pltpu.make_async_copy(source, target, i_sem.at[i])
        for i, (source, target) in enumerate(((src_hbm, src), (routes_hbm, routes), (window_hbm, window)))
    ]
    for c in inputs:
        c.start()
    others = (1, 3, 9, 11, 0, 8, 5, 7, 2, 6, 10)
    count = jnp.int32(0)
    for q in others:
        @pl.when(greets(q))
        def _():
            pl.semaphore_signal(barrier, inc=1, device_id=there(q), device_id_type=pl.DeviceIdType.MESH)
        count = count + greets(q).astype(jnp.int32)

    order = (4, 0, 8, 2, 6, 10, 1, 3, 9, 11, 5, 7)

    def fetch(q):
        return pltpu.make_async_copy(weights.at[q], wv.at[q], w_sem.at[q])

    fetch(4).start()
    for q in order[1:]:
        @pl.when(gets(q))
        def _():
            fetch(q).start()


    inputs[1].wait()
    code = lax.broadcasted_iota(jnp.int32, (16, 128), 0)
    names = jnp.logical_or(routes[0:1, :] == code, routes[1:2, :] == code)
    earlier = lax.broadcasted_iota(jnp.int32, (128, 128), 0) < lax.broadcasted_iota(jnp.int32, (128, 128), 1)
    rank = jnp.dot(
        names.astype(f32).astype(bf16), earlier.astype(f32).astype(bf16), preferred_element_type=f32
    )
    ranked = jnp.where(names, rank, -1.0)
    slot = lax.broadcasted_iota(jnp.int32, (32, 128), 0).astype(f32)
    select = jnp.concatenate(
        [(jnp.broadcast_to(ranked[q : q + 1], (32, 128)) == slot).astype(f32) for q in range(12)], axis=0
    ).astype(bf16)
    inputs[0].wait()
    s32[0:1024, :] = src[...].astype(f32).reshape(1024, 128)
    for f in range(0, 8, 2):
        planes = jnp.concatenate(
            [s32[pl.ds(f + i, 128, stride=8), :].astype(bf16) for i in range(2)], axis=1
        )
        packed = jnp.dot(select, planes, preferred_element_type=f32)
        for i in range(2):
            o32[pl.ds(f + i, 384, stride=8), :] = packed[:, i * 128 : i * 128 + 128]
    for q in range(12):
        sendb[q] = o32[q * 256 : q * 256 + 256, :].astype(bf16)

    spot = lax.broadcasted_iota(jnp.int32, (256, 384), 0)
    wanted = lax.rem(spot, 64) * 4 + lax.div(spot, 64)
    inputs[2].wait()
    lands = jnp.concatenate([window[q] for q in range(12)], axis=1)
    place[...] = (jnp.broadcast_to(lands, (256, 384)) == wanted).astype(f32).astype(bf16)
    pl.semaphore_wait(barrier, count)

    def route(q):
        return pltpu.make_async_remote_copy(
            src_ref=sendb.at[q], dst_ref=recvb.at[q], send_sem=send_sem.at[q], recv_sem=recv_sem.at[q],
            device_id=there(q), device_id_type=pl.DeviceIdType.MESH,
        )

    for q in (2, 6, 10, 1, 3, 0, 8, 9, 11, 5, 7):
        @pl.when(sends(q))
        def _():
            route(q).start()

    zero_rows = jnp.zeros((16, 512), bf16)
    zero_tile = jnp.zeros((16, 128), bf16)
    fe[544:592, :] = jnp.zeros((48, 512), bf16)

    @pl.when(band == 0)
    def _():
        fe[0:16, :] = zero_rows
        ln[...] = zero_tile
        rn[...] = zero_tile

    @pl.when(band == n_band - 1)
    def _():
        fe[528:544, :] = zero_rows
        ls[...] = zero_tile
        rs[...] = zero_tile

    def product(q, held):
        fetch(q).wait()
        for i in range(16):
            col = i * 256
            both = jnp.concatenate([wv[q, col : col + 128, :], wv[q, col + 128 : col + 256, :]], axis=1)
            got = jnp.dot(held[i * 16 : i * 16 + 16, :], both, preferred_element_type=f32)
            c32[q * 256 + i * 16 : q * 256 + i * 16 + 8, :] = got[0:8, 0:128]
            c32[q * 256 + i * 16 + 8 : q * 256 + i * 16 + 16, :] = got[8:16, 128:256]

    product(4, sendb.at[4])
    for q in order[1:]:
        @pl.when(gets(q))
        def _():
            route(q).wait_recv()
            product(q, recvb.at[q])

        @pl.when(jnp.logical_not(gets(q)))
        def _():
            c32[q * 256 : q * 256 + 256, :] = jnp.zeros((256, 128), f32)

    for f in range(0, 8, 2):
        planes = jnp.concatenate(
            [c32[pl.ds(f + i, 384, stride=8), :].astype(bf16) for i in range(2)], axis=1
        )
        summed = jnp.dot(place[...], planes, preferred_element_type=f32)
        for i in range(2):
            for c in range(4):
                fs32[c, pl.ds(f + i, 64, stride=8), :] = summed[
                    c * 64 : c * 64 + 64, i * 128 : i * 128 + 128
                ]
    for c in range(4):
        fe[16:528, c * 128 : c * 128 + 128] = fs32[c, 0:512, :].astype(bf16)

    pick_row = lax.broadcasted_iota(jnp.int32, (16, 128), 0)
    pick_col = lax.broadcasted_iota(jnp.int32, (16, 128), 1)
    pick_left = jnp.logical_and(pick_row == pick_col, pick_row < 2).astype(f32).astype(bf16)
    pick_right = (pick_col == pick_row + 112).astype(f32)
    pick_right = jnp.where(pick_row >= 14, pick_right, 0.0).astype(bf16)
    coll[...] = lax.dot_general(pick_left, fe[16:528, 0:128], NT, preferred_element_type=f32).astype(bf16)
    colr[...] = lax.dot_general(pick_right, fe[16:528, 384:512], NT, preferred_element_type=f32).astype(bf16)

    east, west = lax.rem(lon + 1, n_lon), lax.rem(lon + n_lon - 1, n_lon)
    north, south = band - 1, band + 1

    def halo(i, source, target, b, l):
        return pltpu.make_async_remote_copy(
            src_ref=source, dst_ref=target, send_sem=hs_sem.at[i], recv_sem=hr_sem.at[i],
            device_id={"band": b, "lon": l}, device_id_type=pl.DeviceIdType.MESH,
        )

    up = [
        halo(0, colr.at[:, 0:128], ls, north, east),
        halo(1, coll.at[:, 0:128], rs, north, west),
        halo(2, fe.at[16:32, :], fe.at[528:544, :], north, lon),
    ]
    down = [
        halo(3, colr.at[:, 384:512], ln, south, east),
        halo(4, coll.at[:, 384:512], rn, south, west),
        halo(5, fe.at[512:528, :], fe.at[0:16, :], south, lon),
    ]
    side = [halo(6, colr, lc, band, east), halo(7, coll, rc, band, west)]

    @pl.when(band > 0)
    def _():
        for c in up:
            c.start()

    @pl.when(band < n_band - 1)
    def _():
        for c in down:
            c.start()

    for c in side:
        c.start()

    same = (lax.broadcasted_iota(jnp.int32, (128, 128), 0) == lax.broadcasted_iota(jnp.int32, (128, 128), 1))
    same = same.astype(f32).astype(bf16)
    pad = jnp.zeros((16, 128), bf16)

    def turn(w):
        for t in range(4):
            piece = fe[64 * w : 64 * w + 80, t * 128 : t * 128 + 128]
            turned = lax.dot_general(
                same, jnp.concatenate([piece, piece, piece, pad], axis=0), NT, preferred_element_type=f32
            )
            for i in range(2):
                y32[w, i, 16 + t * 128 : 144 + t * 128, :] = turned[:, i * 128 : i * 128 + 128]

    def shift(w, start, size):
        lane = lax.broadcasted_iota(jnp.int32, (size, 128), 1)
        at = [slice(start + 14 + b, start + 14 + b + size) for b in range(3)]
        low = jnp.where(lane < 80, y32[w, 0, at[0], :], y32[w, 0, at[1], :])
        high = jnp.where(lane < 32, y32[w, 1, at[1], :], y32[w, 1, at[2], :])
        lv[w, start : start + size, 0:128] = low.astype(bf16)
        lv[w, start : start + size, 128:256] = high.astype(bf16)

    def body_out(w):
        return pltpu.make_async_copy(lv.at[w, 16:496, :], out.at[w, 16:496, :], o_sem.at[w])

    def ends_out(i):
        part = (slice(0, 16), slice(496, 528))[i % 2]
        group = (slice(1, 8), slice(0, 1), slice(8, 9))[i // 2]
        return pltpu.make_async_copy(lv.at[group, part, :], out.at[group, part, :], e_sem.at[i])

    for w in range(1, 8):
        turn(w)
        shift(w, 16, 480)
        body_out(w).start()

    def arrive(copies):
        for c in copies:
            c.wait_recv()

    @pl.when(band < n_band - 1)
    def _():
        arrive(up[2:])

    @pl.when(band > 0)
    def _():
        arrive(down[2:])

    for w in (0, 8):
        turn(w)
        shift(w, 16, 480)
        body_out(w).start()

    lane = lax.broadcasted_iota(jnp.int32, (16, 640), 1)
    part = lax.broadcasted_iota(jnp.int32, (16, 256), 1)

    def ends(whole, w):
        first = (whole if w == 0 else pltpu.roll(whole, 640 - 64 * w, 1))[:, 0:256]
        first = jnp.where(part < 80, first, 0.0)
        first = first + pltpu.roll(first, 80, 1) + pltpu.roll(first, 160, 1)
        for i in range(2):
            y32[w, i, 0:16, :] = first[:, i * 128 : i * 128 + 128]
            y32[w, i, 528:544, :] = first[:, i * 128 : i * 128 + 128]
        shift(w, 0, 16)
        shift(w, 496, 32)

    arrive(side)
    mid = lc[...].astype(f32) + rc[...].astype(f32)
    mid = pltpu.roll(jnp.concatenate([mid, jnp.zeros((16, 128), f32)], axis=1), 16, 1)
    for w in range(1, 8):
        ends(mid, w)
    for i in range(2):
        ends_out(i).start()

    @pl.when(band < n_band - 1)
    def _():
        arrive(up[:2])

    @pl.when(band > 0)
    def _():
        arrive(down[:2])

    blank = jnp.zeros((16, 512), f32)
    top = jnp.concatenate([pltpu.roll(ln[...].astype(f32) + rn[...].astype(f32), 16, 1), blank], axis=1)
    low = jnp.concatenate([blank, pltpu.roll(ls[...].astype(f32) + rs[...].astype(f32), 16, 1)], axis=1)
    whole = jnp.where(lane < 16, top, jnp.where(lane < 528, mid, jnp.where(lane < 544, low, 0.0)))
    for w in (0, 8):
        ends(whole, w)
    for i in range(2, 6):
        ends_out(i).start()
    for w in range(9):
        body_out(w).wait()
    for i in range(6):
        ends_out(i).wait()

    for q in others:
        @pl.when(sends(q))
        def _():
            route(q).wait_send()

    @pl.when(band > 0)
    def _():
        for c in up:
            c.wait_send()

    @pl.when(band < n_band - 1)
    def _():
        for c in down:
            c.wait_send()

    for c in side:
        c.wait_send()


def gather(source, routes, window, weights):
    V, D = pltpu.VMEM, pltpu.SemaphoreType.DMA
    bf16, f32 = jnp.bfloat16, jnp.float32
    return pl.pallas_call(
        gather_kernel,
        out_shape=jax.ShapeDtypeStruct((9, 528, 256), bf16),
        in_specs=[pl.BlockSpec(memory_space=pltpu.HBM)] * 4,
        out_specs=pl.BlockSpec(memory_space=pl.ANY),
        scratch_shapes=[
            V((128, 8, 128), bf16), V((2, 128), jnp.int32), V((12, 1, 32), jnp.int32),
            V((12, 4096, 128), bf16), V((1032, 128), f32), V((3080, 128), f32),
            V((12, 256, 128), bf16), V((12, 256, 128), bf16), V((3080, 128), f32),
            V((256, 384), bf16), V((4, 520, 128), f32), V((592, 512), bf16),
            V((16, 512), bf16), V((16, 512), bf16),
            V((16, 512), bf16), V((16, 128), bf16), V((16, 128), bf16),
            V((16, 512), bf16), V((16, 128), bf16), V((16, 128), bf16),
            V((9, 2, 544, 128), f32), V((9, 528, 256), bf16),
            D((12,)), D((12,)), D((12,)), D((8,)), D((8,)), D((9,)), D((6,)), D((3,)),
        ],
        compiler_params=pltpu.CompilerParams(
            collective_id=0, has_side_effects=True, vmem_limit_bytes=40 * 1024 * 1024
        ),
        name="gather",
    )(source, routes, window, weights)


UNROLL = 4
MC = 128
SC = 256

def conv_kernel(lv, sw, sb, mw, mb, out, tmat, ma, ml, mr, h32, r0, r1, r2, r3, h32b, y32, y32b, o0, o1, o2, o3, sems):
    f32, bf16 = jnp.float32, jnp.bfloat16
    band, n_band = lax.axis_index("band"), lax.axis_size("band")

    sw32 = sw[...].astype(f32)
    for j in range(4):
        for y in range(2):
            top = 2 * j + y
            pieces = []
            for b in range(3):
                if top > 0:
                    pieces.append(jnp.zeros((8 * top, 128), f32))
                for a in range(3):
                    pieces.append(sw32[(3 * a + b) * 8 : (3 * a + b) * 8 + 8])
                if top < 7:
                    pieces.append(jnp.zeros((8 * (7 - top), 128), f32))
            pieces.append(jnp.zeros((16, 128), f32))
            tmat[j, :, y * 128 : y * 128 + 128] = jnp.concatenate(pieces, axis=0).astype(bf16)
    for a in range(3):
        row = a * 256
        ma[row : row + 128, 0:128] = mw[3 * a + 1]
        ma[row : row + 128, 128:256] = mw[3 * a]
        ma[row + 128 : row + 256, 0:128] = mw[3 * a + 2]
        ma[row + 128 : row + 256, 128:256] = mw[3 * a + 1]
    for side, b in ((ml, 0), (mr, 2)):
        for r in range(4):
            for o in range(2):
                a = r - o
                block = mw[3 * a + b] if 0 <= a <= 2 else jnp.zeros((128, 128), bf16)
                side[r * 128 : r * 128 + 128, o * 128 : o * 128 + 128] = block

    hb = sb[...] * 0.5
    bias = mb[...]

    def stem(pair, h32, m, size):
        w = pair // 4
        acc = jnp.dot(lv[w, m : m + size], tmat[pair - w * 4], preferred_element_type=f32)
        for y in range(2):
            u = acc[:, y * 128 : y * 128 + 128] * 0.5 + hb
            h = u + u * jnp.tanh(u)
            row = 2 * pair + y
            gone = jnp.logical_or(
                jnp.logical_and(band == 0, row == 0), jnp.logical_and(band == n_band - 1, row == 65)
            )
            h32[y, m : m + size] = h * jnp.where(gone, 0.0, 1.0)

    def split(ring, h32, m, size):
        for y in range(2):
            for i, start in enumerate((1, 2, 0, 3)):
                ring[y, m : m + size, i * 128 : i * 128 + 128] = h32[
                    y, pl.ds(2 * m + start, size, stride=2), :
                ].astype(bf16)

    def mix(lo, hi, ob, y32, m, size):
        rows = [r[k, m : m + size, :] for r in (lo, hi) for k in range(2)]
        left = jnp.dot(
            jnp.concatenate([r[:, 256:384] for r in rows], axis=1), ml[...], preferred_element_type=f32
        )
        right = jnp.dot(
            jnp.concatenate([r[:, 384:512] for r in rows], axis=1), mr[...], preferred_element_type=f32
        )
        for o in range(2):
            both = jnp.dot(
                jnp.concatenate([r[:, 0:256] for r in rows[o : o + 3]], axis=1), ma[...], preferred_element_type=f32
            )
            cut = slice(o * 128, o * 128 + 128)
            y32[o, pl.ds(2 * m, size, stride=2), :] = both[:, 0:128] + left[:, cut] + bias
            y32[o, pl.ds(2 * m + 1, size, stride=2), :] = both[:, 128:256] + right[:, cut] + bias
            ob[o, 2 * m : 2 * m + 2 * size] = y32[o, 2 * m : 2 * m + 2 * size].astype(bf16)

    def both(stem_args, mix_args):
        cuts = [(k * SC, SC if k < 512 // SC - 1 else SC + 8) for k in range(512 // SC)]
        done = 0
        for k in range(256 // MC):
            if mix_args:
                mix(*mix_args, k * MC, MC)
            if stem_args:
                n = len(cuts) * MC // 256
                for m, size in cuts[k * n : k * n + n]:
                    stem(stem_args[0], stem_args[1], m, size)
        if stem_args:
            for k in range(256 // MC):
                split(stem_args[2], stem_args[1], k * MC, MC)

    rings = (r0, r1, r2, r3)
    obs = (o0, o1, o2, o3)
    hs = (h32, h32b)
    ys = (y32, y32b)
    for pair in range(3):
        both((jnp.int32(pair), hs[pair % 2], rings[pair]), None)

    def put(p, i):
        return pltpu.make_async_copy(obs[i], out.at[pl.ds(2 * p, 2)], sems.at[i])

    def step(p, i, stems):
        ahead = (p + 3, hs[(i + 1) % 2], rings[(i + 3) % 4]) if stems else None
        both(ahead, (rings[i], rings[(i + 1) % 4], obs[i], ys[i % 2]))
        put(p, i).start()

    def body(t, carry):
        for i in range(4):
            p = 4 * t + i

            @pl.when(t > 0)
            def _():
                put(p - 4, i).wait()

            step(p, i, True)
        return carry

    lax.fori_loop(0, 7, body, 0)
    for i in range(4):
        put(24 + i, i).wait()
        step(jnp.int32(28 + i), i, i < 2)
    for i in range(4):
        put(28 + i, i).wait()


def conv(lhs, sw, sb, mw, mb):
    V = pltpu.VMEM
    bf16, f32 = jnp.bfloat16, jnp.float32
    vm = pl.BlockSpec(memory_space=pltpu.VMEM)
    return pl.pallas_call(
        conv_kernel,
        out_shape=jax.ShapeDtypeStruct((64, 512, 128), bf16),
        in_specs=[vm] * 5,
        out_specs=pl.BlockSpec(memory_space=pl.ANY),
        scratch_shapes=[
            V((4, 256, 256), bf16), V((768, 256), bf16), V((512, 256), bf16), V((512, 256), bf16),
            V((2, 528, 128), f32),
            V((2, 256, 512), bf16), V((2, 256, 512), bf16), V((2, 256, 512), bf16), V((2, 256, 512), bf16),
            V((2, 520, 128), f32), V((2, 520, 128), f32), V((2, 520, 128), f32),
            V((2, 512, 128), bf16), V((2, 512, 128), bf16), V((2, 512, 128), bf16), V((2, 512, 128), bf16),
            pltpu.SemaphoreType.DMA((4,)),
        ],
        compiler_params=pltpu.CompilerParams(vmem_limit_bytes=24 * 1024 * 1024),
        name="conv",
    )(lhs, sw, sb, mw, mb)


def on_device(source, routes, slot_weights, window, stem_weight, stem_bias, mix_weight, mix_bias):
    operands = (source, routes.T, window.transpose(1, 0, 2), slot_weights.reshape(12, 4096, 128))
    columns = gather(*(pltpu.with_memory_space_constraint(x, pltpu.HBM) for x in operands))
    return conv(
        columns,
        stem_weight.reshape(72, 128),
        stem_bias.reshape(1, 128),
        mix_weight,
        mix_bias.reshape(1, 128),
    )


def solution(mesh):
    in_specs = (
        P(("band", "lon"), None, None),
        P(("band", "lon"), None),
        P(("band", "lon"), None, None, None, None),
        P(("band", "lon"), None, None),
        P(),
        P(),
        P(),
        P(),
    )
    out_specs = P("band", "lon", None)
    return jax.shard_map(
        on_device, mesh=mesh, in_specs=in_specs, out_specs=out_specs, check_vma=False
    )
```
